512 devices in a mesh: ctx: 64 (over x, z, core), head: 8 (over y).
Axes of the slice: x: 4, y: 8, z: 8, core: 2. Of those that a mesh axis runs over, the one named last changes fastest.
Arguments:
- queries: bfloat16 [8192, 4096], P('ctx', 'head'), may hold values from -80 to 80
- keys: bfloat16 [8192, 1024], P('ctx', 'head'), may hold values from -80 to 80
- values: bfloat16 [8192, 1024], P('ctx', 'head'), may hold values from -6 to 6
- feat_q: bfloat16 [32, 128, 64], P('head'), may hold values from -1 to 1
- feat_k: bfloat16 [32, 128, 64], P('head'), may hold values from -1 to 1
Outputs:
- student: bfloat16 [8192, 4096], P('ctx', 'head')
- grad_q: float32 [32, 128, 64], P('head')
- grad_k: float32 [32, 128, 64], P('head')
- mean_error: float32 [], replicated
The draws below stay inside these ranges and needn't reach their ends.
All inputs are finite; a program needn't handle non-finite values.
Results may differ from the reference program's by a relative error of at most 0.007.
The reference program's roundings to bfloat16 on the way count: a program that leaves them out, or rounds other values in their place, can miss the bound.
Values may be sent and summed in bfloat16 or wider, within the bound.
No kernel may reach another device: no remote copies, remote signals or barrier semaphores. Data moves between devices by JAX's collectives and lax.ppermute only.
A program may use at most 128 MiB of HBM per device.

```python
import jax
import jax.numpy as jnp
from jax import lax

HD = 128
FEAT = 64
TOK_DEV = 128
KV_HEADS = 8
HEADS = 32
SEQ = 8192


def drawn_pair(key):
    base_k = jax.random.normal(jax.random.fold_in(key, 1), (SEQ, KV_HEADS, HD), jnp.float32)
    base_q = jax.random.normal(jax.random.fold_in(key, 2), (SEQ, HEADS, HD), jnp.float32)
    base_q = jnp.clip(base_q, -80.0, 80.0)
    base_k = jnp.clip(base_k, -80.0, 80.0)
    return (base_q.reshape(SEQ, HEADS * HD), base_k.reshape(SEQ, KV_HEADS * HD))


def draw_queries(key, part):
    return drawn_pair(key)[0].astype(jnp.bfloat16)


def draw_keys(key, part):
    return drawn_pair(key)[1].astype(jnp.bfloat16)


def shard_levels(key, dims, pieces, low, largest):
    loudness = 1.0
    for position, shards_of in pieces:
        draws = jax.random.uniform(jax.random.fold_in(jax.random.fold_in(key, 6), position), (shards_of,), jnp.float32, low / len(pieces), largest / len(pieces))
        loudness = loudness * jnp.repeat(jnp.exp(draws), dims[position] // shards_of).reshape((-1,) + (1,) * (len(dims) - 1 - position))
    return loudness


def normal_values(key, shape, spread, most, pieces=(), kind=jnp.bfloat16):
    gain = shard_levels(key, shape, pieces, -0.22, 0.18) if pieces else 1.0
    result = jax.random.normal(key, shape, jnp.float32) * spread * gain
    return jnp.minimum(jnp.maximum(result, -most), most).astype(kind)


def setup_inputs(seed: int = 0) -> dict:
    arg_keys = jax.random.split(jax.random.key(seed), 6)
    queries = draw_queries(jax.random.fold_in(arg_keys[5], 71), 0)
    keys = draw_keys(jax.random.fold_in(arg_keys[5], 71), 0)
    values = normal_values(arg_keys[2], (SEQ, KV_HEADS * HD), 1.0, 6.0, ((0, 64), (1, 8)))
    feat_q = normal_values(arg_keys[3], (HEADS, HD, FEAT), (HD // 4) ** -0.5, 1.0, ((0, 8),))
    feat_k = normal_values(arg_keys[4], (HEADS, HD, FEAT), (HD // 4) ** -0.5, 1.0, ((0, 8),))
    return {"queries": queries, "keys": keys, "values": values, "feat_q": feat_q, "feat_k": feat_k}


precise_scores = lax.Precision.HIGHEST

def rounded_weights(array):
    return lax.optimization_barrier(array.astype(jnp.bfloat16)).astype(jnp.float32)

def feature_map(inputs, weight):
    logits = jnp.einsum('nhd,hdf->nhf', inputs, weight, precision=precise_scores)
    positive = jax.nn.softmax(logits, axis=-1)
    negative = jax.nn.softmax(-logits, axis=-1)
    return (positive, negative, rounded_weights(jnp.concatenate([positive, negative], axis=-1)))

def feature_grad(positive, negative, upstream):
    width = positive.shape[-1]
    up_pos = upstream[..., :width]
    up_neg = upstream[..., width:]
    return positive * (up_pos - lax.optimization_barrier(jnp.sum(up_pos * positive, axis=-1, keepdims=True))) - negative * (up_neg - lax.optimization_barrier(jnp.sum(up_neg * negative, axis=-1, keepdims=True)))

def reference(queries, keys, values, feat_q, feat_k):
    seq_len = queries.shape[0]
    head_count = feat_q.shape[0]
    head_dim = feat_q.shape[1]
    group_size = head_count // KV_HEADS
    block_length = TOK_DEV
    block_count = seq_len // block_length

    def spread_heads(array):
        widened = jnp.repeat(array.astype(jnp.float32).reshape(seq_len, KV_HEADS, head_dim), group_size, axis=1)
        return widened.reshape(block_count, block_length, head_count, head_dim)
    query_blocks = queries.astype(jnp.float32).reshape(block_count, block_length, head_count, head_dim)
    key_block_list = spread_heads(keys)
    value_block_list = spread_heads(values)
    weight_q = feat_q.astype(jnp.float32)
    weight_k = feat_k.astype(jnp.float32)
    logit_scale = head_dim ** (-0.5)
    block_offsets = jnp.arange(block_length, dtype=jnp.int32)

    def teacher_block(block_id):
        current_query = query_blocks[block_id]
        query_pos = block_id * block_length + block_offsets

        def absorb_block(key_index, partial_value_sum):
            running, totals, accumulated_output = partial_value_sum
            score_matrix = jnp.einsum('jlx,ulx->jlu', current_query, key_block_list[key_index], precision=precise_scores) * logit_scale
            key_positions = key_index * block_length + block_offsets
            allowed = (query_pos[:, None] >= key_positions[None, :])[:, None, :]
            score_matrix = jnp.where(allowed, score_matrix, -1e+30)
            new_max = jnp.maximum(running, lax.optimization_barrier(jnp.max(score_matrix, axis=-1)))
            attention_weights = jnp.where(allowed, jnp.exp(score_matrix - new_max[..., None]), 0.0)
            rescale_factor = jnp.exp(running - new_max)
            totals = totals * rescale_factor + lax.optimization_barrier(jnp.sum(attention_weights, axis=-1))
            accumulated_output = accumulated_output * rescale_factor[..., None] + jnp.einsum('uja,ajt->ujt', rounded_weights(attention_weights), value_block_list[key_index], precision=precise_scores)
            return (new_max, totals, accumulated_output)
        initial = (jnp.full((block_length, head_count), -1e+30, jnp.float32), jnp.zeros((block_length, head_count), jnp.float32), jnp.zeros((block_length, head_count, head_dim), jnp.float32))
        running, totals, accumulated_output = lax.fori_loop(0, block_id + 1, absorb_block, initial)
        return accumulated_output / totals[..., None]
    teacher = lax.map(teacher_block, jnp.arange(block_count, dtype=jnp.int32))
    causal = block_offsets[:, None] >= block_offsets[None, :]
    fdim2 = 2 * weight_q.shape[2]

    def forward(partial_value_sum, inputs):
        state, norm, grad_query, error = partial_value_sum
        current_query, key_now, value_now, teacher_now = inputs
        pos_q, neg_q, feat_query = feature_map(current_query, weight_q)
        pos_k, neg_k, feat_key = feature_map(key_now, weight_k)
        amat = jnp.einsum('ihf,jhf->hij', feat_query, feat_key, precision=precise_scores)
        amat = jnp.where(causal[None], amat, 0.0)
        numer = jnp.einsum('hij,jhd->ihd', rounded_weights(amat), value_now, precision=precise_scores) + jnp.einsum('ihf,hfd->ihd', feat_query, state, precision=precise_scores)
        denom = lax.optimization_barrier(jnp.sum(amat, axis=-1)).T + jnp.einsum('ihf,hf->ih', feat_query, norm, precision=precise_scores)
        output = numer / denom[..., None]
        diff = output - teacher_now
        error = error + jnp.sum(diff * diff)
        grad_out = 2.0 * diff
        grad_numer = grad_out / denom[..., None]
        grad_denom = -lax.optimization_barrier(jnp.sum(grad_out * output, axis=-1)) / denom
        numer_bf = rounded_weights(grad_numer)
        grad_mat = jnp.einsum('ihd,jhd->hij', numer_bf, value_now, precision=precise_scores) + grad_denom.T[:, :, None]
        grad_mat = rounded_weights(jnp.where(causal[None], grad_mat, 0.0))
        grad_fq = jnp.einsum('hij,jhf->ihf', grad_mat, feat_key, precision=precise_scores) + jnp.einsum('ihd,hfd->ihf', grad_numer, state, precision=precise_scores) + grad_denom[..., None] * norm[None]
        grad_logit = rounded_weights(feature_grad(pos_q, neg_q, grad_fq))
        grad_query = grad_query + jnp.einsum('bhd,bhf->hdf', current_query, grad_logit, precision=precise_scores)
        local_fk = jnp.einsum('hij,ihf->jhf', grad_mat, feat_query, precision=precise_scores)
        local_state = jnp.einsum('ihf,ihd->hfd', feat_query, numer_bf, precision=precise_scores)
        local_norm = jnp.einsum('ihf,ih->hf', feat_query, grad_denom, precision=precise_scores)
        state = state + jnp.einsum('jhf,jhd->hfd', feat_key, value_now, precision=precise_scores)
        norm = norm + lax.optimization_barrier(jnp.sum(feat_key, axis=0))
        return ((state, norm, grad_query, error), (output.astype(jnp.bfloat16), local_fk, local_state, local_norm))
    start_fwd = (jnp.zeros((head_count, fdim2, head_dim), jnp.float32), jnp.zeros((head_count, fdim2), jnp.float32), jnp.zeros(weight_q.shape, jnp.float32), jnp.zeros((), jnp.float32))
    finals, stacked = lax.scan(forward, start_fwd, (query_blocks, key_block_list, value_block_list, teacher))
    grad_query = finals[2]
    error = finals[3]
    outputs, local_fks, local_states, local_norms = stacked

    def backward(partial_value_sum, inputs):
        later_state, later_norm, grad_key = partial_value_sum
        key_now, value_now, local_fk, local_state, local_norm = inputs
        pos_k, neg_k, feat_key = feature_map(key_now, weight_k)
        grad_fk = local_fk + jnp.einsum('hfd,jhd->jhf', later_state, value_now, precision=precise_scores) + later_norm[None]
        grad_logit = rounded_weights(feature_grad(pos_k, neg_k, grad_fk))
        grad_key = grad_key + jnp.einsum('jhd,jhf->hdf', key_now, grad_logit, precision=precise_scores)
        return ((later_state + local_state, later_norm + local_norm, grad_key), None)
    start_back = (jnp.zeros((head_count, fdim2, head_dim), jnp.float32), jnp.zeros((head_count, fdim2), jnp.float32), jnp.zeros(weight_k.shape, jnp.float32))
    back_final, unused = lax.scan(backward, start_back, (key_block_list, value_block_list, local_fks, local_states, local_norms), reverse=True)
    student = outputs.reshape(seq_len, head_count * head_dim)
    mean_error = error / (seq_len * head_count * head_dim)
    return (student, grad_query, back_final[2], mean_error)
```

```python
import functools

import jax
import jax.numpy as jnp
from jax import lax
from jax.experimental import pallas as pl
from jax.experimental.pallas import tpu as pltpu
from jax.sharding import Mesh
from jax.sharding import PartitionSpec as P

CTX = ("x", "z", "c")
BF = jnp.bfloat16
F32 = jnp.float32
NEG = -1e30
LOG2E = 1.4426950408889634
EXT = 16


def dot(a, b):
    return lax.dot_general(a, b, (((1,), (0,)), ((), ())), preferred_element_type=F32)


def dot_t(a, b):
    return lax.dot_general(a, b, (((1,), (1,)), ((), ())), preferred_element_type=F32)


def flip(a):
    return a.astype(F32).T


def pieces(a, count):
    out = []
    for _ in range(count):
        top = a.astype(BF)
        out.append(top)
        a = a - top.astype(F32)
    return out


def halves(logits):
    high = jnp.max(logits, axis=0, keepdims=True)
    low = jnp.min(logits, axis=0, keepdims=True)
    up = jnp.exp(logits - high)
    down = jnp.exp(low - logits)
    up = up * (1.0 / jnp.sum(up, axis=0, keepdims=True))
    down = down * (1.0 / jnp.sum(down, axis=0, keepdims=True))
    return up, down


def half_grad(p, d):
    return p * (d - jnp.sum(d * p, axis=0, keepdims=True))


def whole(*shape_dtype):
    return pl.BlockSpec(memory_space=pltpu.VMEM)


SM = pl.BlockSpec(memory_space=pltpu.SMEM)


def call(kernel, outs, ins, n_smem=0, scratch=(), aliases=None):
    vm = pl.BlockSpec(memory_space=pltpu.VMEM)
    return pl.pallas_call(
        kernel,
        out_shape=[jax.ShapeDtypeStruct(s, d) for s, d in outs],
        in_specs=[SM] * n_smem + [vm] * (len(ins) - n_smem),
        out_specs=[vm] * len(outs),
        scratch_shapes=list(scratch),
        input_output_aliases=aliases or {},
        compiler_params=pltpu.CompilerParams(vmem_limit_bytes=56 * 1024 * 1024),
    )(*ins)


def prep_kernel(q_ref, k_ref, v_ref, qt_ref, kv_ref):
    heads = q_ref.shape[1] // 128
    for h in range(heads):
        qt_ref[:, h * 128 : (h + 1) * 128] = flip(q_ref[:, h * 128 : (h + 1) * 128]).astype(BF)
    k = k_ref[...]
    vt = flip(v_ref[...]).astype(BF)
    for i in range(kv_ref.shape[0]):
        kv_ref[i, 0] = k
        kv_ref[i, 1] = vt


def load_chunk(kv_ref, lead, first, cb):
    kc = kv_ref[(*lead, pl.ds(first, cb), 0)].reshape(cb * 128, 128)
    vt = jnp.concatenate([kv_ref[(*lead, first + b, 1)] for b in range(cb)], axis=1)
    return kc, vt


def attend_chunk(kc, vt, q_refs, m_ref, l_ref, o_ref, c1, mask=None):
    at = 0
    for qi, q_ref in enumerate(q_refs):
        width = q_ref.shape[1]
        step = min(256, width)
        for t in range(0, width, step):
            cols = slice(at, at + step)
            st = dot(kc, q_ref[:, t : t + step])
            if mask is not None:
                ok = mask(qi, st.shape)
                st = jnp.where(ok, st, NEG)
            m_old = m_ref[:, cols]
            m_new = jnp.maximum(m_old, jnp.max(st, axis=0, keepdims=True))
            p = jnp.exp2((st - m_new) * c1)
            if mask is not None:
                p = jnp.where(ok, p, 0.0)
            alpha = jnp.exp2((m_old - m_new) * c1)
            m_ref[:, cols] = m_new
            l_ref[:, cols] = l_ref[:, cols] * alpha + jnp.sum(p, axis=0, keepdims=True)
            o_ref[:, cols] = o_ref[:, cols] * alpha + dot(vt, p.astype(BF))
            at += step


def state_chunk(kc, vt, wk, st_ref, put, keep=None):
    heads = wk.shape[0] // 64
    logits = dot_t(wk, kc)
    feats = []
    for h in range(heads):
        up, down = halves(logits[h * 64 : (h + 1) * 64])
        put(h, up, down)
        feats += [up, down]
    feat = jnp.concatenate(feats, axis=0)
    if keep is not None:
        feat = jnp.where(keep(feat.shape), feat, 0.0)
    vext = jnp.concatenate([vt, jnp.ones((EXT, vt.shape[1]), BF)], axis=0)
    st_ref[...] += dot_t(vext, feat.astype(BF))


def own_kernel(c1, cb, idx_ref, qt_ref, qp_ref, fk_ref, kv_ref, m_ref, l_ref, o_ref, st_ref, pk_ref, wk_ref):
    z, c = idx_ref[1], idx_ref[2]
    nz = kv_ref.shape[0]
    heads = fk_ref.shape[0]
    for h in range(heads):
        wk_ref[h * 64 : (h + 1) * 64, :] = flip(fk_ref[h]).astype(BF)
    m_ref[...] = jnp.full(m_ref.shape, NEG, F32)
    l_ref[...] = jnp.zeros(l_ref.shape, F32)
    o_ref[...] = jnp.zeros(o_ref.shape, F32)
    st_ref[...] = jnp.zeros(st_ref.shape, F32)

    def chunk(i, carry):
        first = i * cb
        kc, vt = load_chunk(kv_ref, (), first, cb)

        def mask(qi, shape):
            row = lax.broadcasted_iota(jnp.int32, shape, 0)
            kpos = (2 * (first + row // 128) + c) * 128 + row % 128
            col = lax.broadcasted_iota(jnp.int32, shape, 1)
            qpos = (2 * z + (c if qi == 0 else 1 - c)) * 128 + col % 128
            return kpos <= qpos

        attend_chunk(kc, vt, (qt_ref, qp_ref), m_ref, l_ref, o_ref, c1, mask)

        def put(h, up, down):
            for b in range(cb):
                pk_ref[first + b, h * 128 : h * 128 + 64, :] = up[:, b * 128 : (b + 1) * 128]
                pk_ref[first + b, h * 128 + 64 : (h + 1) * 128, :] = down[:, b * 128 : (b + 1) * 128]

        def keep(shape):
            col = lax.broadcasted_iota(jnp.int32, shape, 1)
            return first + col // 128 < z

        state_chunk(kc, vt, wk_ref[...], st_ref, put, keep)
        return carry

    lax.fori_loop(0, z // cb + 1, chunk, 0)


def rest_kernel(
    c1, cb, idx_ref, qt_ref, qp_ref, wk_ref, kv_ref, mi_ref, li_ref, oi_ref, si_ref, pown_ref, vown_ref,
    keep_ref, send_ref, pk_ref, m_ref, l_ref, o_ref, st_ref,
):
    x, z, c = idx_ref[0], idx_ref[1], idx_ref[2]
    nz = kv_ref.shape[1]
    per = nz // cb
    m_ref[...] = mi_ref[...]
    l_ref[...] = li_ref[...]
    o_ref[...] = oi_ref[...]
    st_ref[...] = si_ref[...]

    def chunk(i, carry):
        s, first = i // per, (i % per) * cb
        kc, vt = load_chunk(kv_ref, (s,), first, cb)
        attend_chunk(kc, vt, (qt_ref, qp_ref), m_ref, l_ref, o_ref, c1)

        def put(h, up, down):
            for b in range(cb):
                pk_ref[s, first + b, h * 128 : h * 128 + 64, :] = up[:, b * 128 : (b + 1) * 128]
                pk_ref[s, first + b, h * 128 + 64 : (h + 1) * 128, :] = down[:, b * 128 : (b + 1) * 128]

        state_chunk(kc, vt, wk_ref[...], st_ref, put)
        return carry

    lax.fori_loop(0, x * per, chunk, 0)
    half = qt_ref.shape[1]
    rows = st_ref.shape[0]
    keep_ref[0:128] = o_ref[:, :half]
    send_ref[0:128] = o_ref[:, half:]
    pad = jnp.zeros((6, half), F32)
    keep_ref[128:136] = jnp.concatenate([m_ref[:, :half], l_ref[:, :half], pad], axis=0)
    send_ref[128:136] = jnp.concatenate([m_ref[:, half:], l_ref[:, half:], pad], axis=0)
    keep_ref[136 : 136 + rows] = st_ref[...]
    vext = jnp.concatenate([vown_ref[...], jnp.ones((EXT, 128), BF)], axis=0)
    own = dot_t(vext, pown_ref[z].astype(BF))
    send_ref[136 : 136 + rows] = st_ref[...] + jnp.where(c == 0, own, 0.0)


def local_kernel(
    c1, mine_ref, got_ref, qt_ref, q_ref, k_ref, kv_ref, fq_ref, fk_ref,
    y_ref, gq_ref, s_ref, dfk_ref, pk_ref, err_ref,
):
    heads = fq_ref.shape[0]
    rows = 128 + EXT
    k, vt = k_ref[...], kv_ref[...]
    v = flip(vt).astype(BF)
    ri = lax.broadcasted_iota(jnp.int32, (128, 128), 0)
    ci = lax.broadcasted_iota(jnp.int32, (128, 128), 1)
    causal = ri <= ci
    ext_row = lax.broadcasted_iota(jnp.int32, (128, 128), 0)
    total = jnp.zeros((128, 128), F32)
    for h in range(heads):
        cols = slice(h * 128, (h + 1) * 128)
        ma, la = mine_ref[128:129, cols], mine_ref[129:130, cols]
        mb, lb = got_ref[128:129, cols], got_ref[129:130, cols]
        m = jnp.maximum(ma, mb)
        wa, wb = jnp.exp2((ma - m) * c1), jnp.exp2((mb - m) * c1)
        teacher = (mine_ref[0:128, cols] * wa + got_ref[0:128, cols] * wb) / (la * wa + lb * wb)
        state = mine_ref[136 : 136 + rows, cols] + got_ref[136 : 136 + rows, cols]
        qt = qt_ref[:, cols]
        uq, dq = halves(dot(flip(fq_ref[h]).astype(BF), qt))
        uk, dk = halves(dot_t(flip(fk_ref[h]).astype(BF), k))
        pk_ref[h * 128 : h * 128 + 64] = uk
        pk_ref[h * 128 + 64 : (h + 1) * 128] = dk
        fq32 = jnp.concatenate([uq, dq], axis=0)
        fk32 = jnp.concatenate([uk, dk], axis=0)
        fq, fk = fq32.astype(BF), fk32.astype(BF)
        fkj = flip(fk).astype(BF)
        amat = jnp.where(causal, dot(fkj, fq), 0.0)
        s1, s2, s3 = pieces(state, 3)
        prior = dot(s1, fq) + (dot(s2, fq) + dot(s3, fq))
        numer = dot(vt, amat.astype(BF)) + prior[0:128]
        denom = jnp.sum(amat, axis=0, keepdims=True) + prior[128:129]
        y = numer / denom
        y_ref[:, cols] = y.T.astype(BF)
        diff = y - teacher
        total = total + diff * diff
        dy = 2.0 * diff
        dnum = dy / denom
        dden = -jnp.sum(dy * y, axis=0, keepdims=True) / denom
        dnb = dnum.astype(BF)
        dmat = jnp.where(causal, dot(v, dnb) + dden, 0.0).astype(BF)
        t32 = state[0:128].T
        n32 = jnp.broadcast_to(state[128:129], (128, 128)).T
        t1, t2 = pieces(t32, 2)
        d1, d2 = pieces(dnum, 2)
        dfq = dot(fk, dmat) + (dot(t1, d1) + (dot(t1, d2) + dot(t2, d1))) + n32 * dden
        dfk_ref[h * 128 : (h + 1) * 128] = dot_t(fq, dmat)
        e1, e2, e3 = pieces(jnp.broadcast_to(dden, (EXT, 128)), 3)
        s_ref[0:128, cols] = dot_t(dnb, fq)
        s_ref[128 : 128 + EXT, cols] = dot_t(e1, fq) + (dot_t(e2, fq) + dot_t(e3, fq))
        dl = half_grad(uq, dfq[0:64]) - half_grad(dq, dfq[64:128])
        gq_ref[h * 64 : (h + 1) * 64] = dot(dl.astype(BF), q_ref[:, cols])
    err = jnp.sum(jnp.sum(total, axis=0, keepdims=True), axis=1, keepdims=True)
    err_ref[...] = jnp.broadcast_to(err.reshape(1, 1, 1), err_ref.shape)


def later_kernel(
    cb, idx_ref, s_ref, sp_ref, dfk_ref, pown_ref, k_ref, vt_ref, kz_ref, pz_ref, kx_ref, px_ref, gq_ref,
    keep_ref, send_ref, g_ref, w_ref, n_ref,
):
    x, z, c = idx_ref[0], idx_ref[1], idx_ref[2]
    heads = dfk_ref.shape[0] // 128
    nz = kz_ref.shape[0]
    per = nz // cb
    for h in range(heads):
        cols = slice(h * 128, (h + 1) * 128)
        w_ref[cols, 0:128] = s_ref[0:128, cols].T.astype(BF)
        w_ref[cols, 128:256] = sp_ref[0:128, cols].T.astype(BF)
        n_ref[cols] = jnp.broadcast_to(s_ref[128:129, cols] + sp_ref[128:129, cols], (128, 128)).T
    vt, k = vt_ref[...], k_ref[...]
    parts = []
    for h in range(heads):
        cols = slice(h * 128, (h + 1) * 128)
        n_par = jnp.broadcast_to(sp_ref[128:129, cols], (128, 128)).T
        extra = dot(w_ref[cols, 128:256], vt) + n_par
        dfk = dfk_ref[cols] + jnp.where(c == 0, extra, 0.0)
        up, down = pown_ref[h * 128 : h * 128 + 64], pown_ref[h * 128 + 64 : (h + 1) * 128]
        parts.append(half_grad(up, dfk[0:64]) - half_grad(down, dfk[64:128]))
    g_ref[...] = dot(jnp.concatenate(parts, axis=0).astype(BF), k)

    def term(kc, vc, p_at, keep=None):
        v2 = jnp.concatenate([vc, vc], axis=0)
        out = []
        for h in range(heads):
            cols = slice(h * 128, (h + 1) * 128)
            bias = n_ref[cols]
            dfk = dot(w_ref[cols, :], v2) + jnp.concatenate([bias] * cb, axis=1)
            up = jnp.concatenate([p_at(b, slice(h * 128, h * 128 + 64)) for b in range(cb)], axis=1)
            down = jnp.concatenate([p_at(b, slice(h * 128 + 64, (h + 1) * 128)) for b in range(cb)], axis=1)
            out.append(half_grad(up, dfk[0:64]) - half_grad(down, dfk[64:128]))
        dl = jnp.concatenate(out, axis=0)
        if keep is not None:
            dl = jnp.where(keep(dl.shape), dl, 0.0)
        g_ref[...] += dot(dl.astype(BF), kc)

    def own_slice(i, carry):
        first = i * cb
        kc, vc = load_chunk(kz_ref, (), first, cb)

        def keep(shape):
            col = lax.broadcasted_iota(jnp.int32, shape, 1)
            return first + col // 128 < z

        term(kc, vc, lambda b, sl: pz_ref[first + b, sl, :], keep)
        return carry

    lax.fori_loop(0, (z + cb - 1) // cb, own_slice, 0)

    def earlier(i, carry):
        s, first = i // per, (i % per) * cb
        kc, vc = load_chunk(kx_ref, (s,), first, cb)
        term(kc, vc, lambda b, sl: px_ref[s, first + b, sl, :])
        return carry

    lax.fori_loop(0, x * per, earlier, 0)

    @pl.when(c == 0)
    def _():
        keep_ref[...] = gq_ref[...]
        send_ref[...] = g_ref[...]

    @pl.when(c != 0)
    def _():
        keep_ref[...] = g_ref[...]
        send_ref[...] = gq_ref[...]


def last_kernel(count, idx_ref, mine_ref, got_ref, err_ref, gq_ref, gk_ref, e_ref):
    c = idx_ref[2]
    heads = gq_ref.shape[0]

    def put(first, second):
        for h in range(heads):
            gq_ref[h] = first[h * 64 : (h + 1) * 64, :].T
            gk_ref[h] = second[h * 64 : (h + 1) * 64, :].T

    @pl.when(c == 0)
    def _():
        put(mine_ref, got_ref)

    @pl.when(c != 0)
    def _():
        put(got_ref, mine_ref)

    e_ref[...] = err_ref[...] / count


def on_device(queries, keys, values, feat_q, feat_k):
    rows = queries.shape[0]
    heads = feat_q.shape[0]
    hd = keys.shape[1]
    nx, nz = lax.axis_size("x"), lax.axis_size("z")
    nh = lax.axis_size("head")
    n = nx * nz
    cb = min(4, nz)
    cx, cz, cc = lax.axis_index("x"), lax.axis_index("z"), lax.axis_index("c")
    idx = jnp.stack([cx, cz, cc]).astype(jnp.int32)
    c1 = hd**-0.5 * LOG2E
    wide = heads * 128
    srows = 128 + EXT
    swap = lambda a: lax.ppermute(a, "c", [(0, 1), (1, 0)])

    qt, kv = call(
        prep_kernel,
        [((hd, wide), BF), ((nz, 2, 128, 128), BF)],
        (queries, keys, values),
    )
    vt = kv[0, 1]
    kvz = lax.all_to_all(kv, "z", 0, 0, tiled=True)
    qp = swap(qt)
    m, l, o, st, pz, wk = call(
        functools.partial(own_kernel, c1, cb),
        [
            ((1, 2 * wide), F32),
            ((1, 2 * wide), F32),
            ((hd, 2 * wide), F32),
            ((srows, wide), F32),
            ((nz, wide, 128), F32),
            ((heads * 64, 128), BF),
        ],
        (idx, qt, qp, feat_k, kvz),
        n_smem=1,
    )
    kvx = lax.all_to_all(jnp.broadcast_to(kvz[None], (nx, *kvz.shape)), "x", 0, 0, tiled=True)
    mine, send, px = call(
        functools.partial(rest_kernel, c1, cb),
        [
            ((136 + srows, wide), F32),
            ((136 + srows, wide), F32),
            ((nx, nz, wide, 128), F32),
        ],
        (idx, qt, qp, wk, kvx, m, l, o, st, pz, vt),
        n_smem=1,
        scratch=[
            pltpu.VMEM((1, 2 * wide), F32),
            pltpu.VMEM((1, 2 * wide), F32),
            pltpu.VMEM((hd, 2 * wide), F32),
            pltpu.VMEM((srows, wide), F32),
        ],
    )
    got = swap(send)
    student, gq, s, dfk, pown, err = call(
        functools.partial(local_kernel, c1),
        [
            ((rows, wide), BF),
            ((heads * 64, 128), F32),
            ((srows, wide), F32),
            ((wide, 128), F32),
            ((wide, 128), F32),
            ((nh, 8, 128), F32),
        ],
        (mine, got, qt, queries, keys, vt, feat_q, feat_k),
    )
    sp = swap(s)
    err_h = lax.all_to_all(err, "head", 0, 0, tiled=True)
    keep, send = call(
        functools.partial(later_kernel, cb),
        [((heads * 64, 128), F32), ((heads * 64, 128), F32)],
        (idx, s, sp, dfk, pown, keys, vt, kvz, pz, kvx, px, gq),
        n_smem=1,
        scratch=[
            pltpu.VMEM((heads * 64, 128), F32),
            pltpu.VMEM((wide, 256), BF),
            pltpu.VMEM((wide, 128), F32),
        ],
    )
    both = keep + swap(send)
    part = both.reshape(n, heads * 64 // n, 128)
    e_row = jnp.broadcast_to(jnp.sum(err_h[:, 0, :], axis=0)[None, None], (n, 1, 128))
    arrived = lax.all_to_all(jnp.concatenate([part, e_row], axis=1), ("x", "z"), 0, 0, tiled=True)
    summed = jnp.sum(arrived, axis=0)
    out = jnp.broadcast_to(summed[None], (n, *summed.shape))
    out = lax.all_to_all(out, ("x", "z"), 0, 0, tiled=True)
    full = out[:, :-1].reshape(heads * 64, 128)
    e_all = jnp.broadcast_to(out[0, -1:, :], (8, 128))
    return student, full, e_all, idx


def finish(student, full, e_all, idx, heads, count):
    swap = lambda a: lax.ppermute(a, "c", [(0, 1), (1, 0)])
    mine = jnp.concatenate([full, e_all], axis=0)
    got = swap(mine)
    gq, gk, e = call(
        functools.partial(last_kernel, count),
        [((heads, 128, 64), F32), ((heads, 128, 64), F32), ((8, 128), F32)],
        (idx, full, got, e_all + got[heads * 64 :]),
        n_smem=1,
    )
    return student, gq, gk, e[0, 0]


def body(queries, keys, values, feat_q, feat_k):
    heads = feat_q.shape[0]
    n_all = 1
    for a in ("x", "z", "c", "head"):
        n_all *= lax.axis_size(a)
    count = float(n_all * queries.size)
    return finish(*on_device(queries, keys, values, feat_q, feat_k), heads, count)


def solution(mesh):
    nh = mesh.shape["head"]
    nctx = mesh.shape["ctx"]
    nx = 4 if nctx == 64 else 2
    split = Mesh(mesh.devices.reshape(nx, nctx // nx // 2, 2, nh), ("x", "z", "c", "head"))
    in_specs = (
        P(CTX, "head"),
        P(CTX, "head"),
        P(CTX, "head"),
        P("head", None, None),
        P("head", None, None),
    )
    out_specs = (P(CTX, "head"), P("head", None, None), P("head", None, None), P())
    return jax.shard_map(body, mesh=split, in_specs=in_specs, out_specs=out_specs, check_vma=False)
```

```python
import functools

import jax
import jax.numpy as jnp
from jax import lax
from jax.experimental import pallas as pl
from jax.experimental.pallas import tpu as pltpu
from jax.sharding import Mesh
from jax.sharding import PartitionSpec as P

CTX = ("x", "z", "c")
BF = jnp.bfloat16
F32 = jnp.float32
NEG = -1e30
LOG2E = 1.4426950408889634
EXT = 16


def dot(a, b):
    return lax.dot_general(a, b, (((1,), (0,)), ((), ())), preferred_element_type=F32)


def dot_t(a, b):
    return lax.dot_general(a, b, (((1,), (1,)), ((), ())), preferred_element_type=F32)


def flip(a):
    return a.astype(F32).T


def pieces(a, count):
    out = []
    for _ in range(count):
        top = a.astype(BF)
        out.append(top)
        a = a - top.astype(F32)
    return out


def halves(logits):
    high = jnp.max(logits, axis=0, keepdims=True)
    low = jnp.min(logits, axis=0, keepdims=True)
    up = jnp.exp(logits - high)
    down = jnp.exp(low - logits)
    up = up * (1.0 / jnp.sum(up, axis=0, keepdims=True))
    down = down * (1.0 / jnp.sum(down, axis=0, keepdims=True))
    return up, down


def half_grad(p, d):
    return p * (d - jnp.sum(d * p, axis=0, keepdims=True))


def head_rows(h):
    return slice(h * 128, h * 128 + 64), slice(h * 128 + 64, (h + 1) * 128)


def call(kernel, outs, ins, n_smem=0, scratch=(), mib=16):
    vm = pl.BlockSpec(memory_space=pltpu.VMEM)
    sm = pl.BlockSpec(memory_space=pltpu.SMEM)
    return pl.pallas_call(
        kernel,
        out_shape=[jax.ShapeDtypeStruct(s, d) for s, d in outs],
        in_specs=[sm] * n_smem + [vm] * (len(ins) - n_smem),
        out_specs=[vm] * len(outs),
        scratch_shapes=list(scratch),
        compiler_params=pltpu.CompilerParams(vmem_limit_bytes=mib * 1024 * 1024),
    )(*ins)


def prep_kernel(q_ref, k_ref, v_ref, qt_ref, kv_ref, vt_ref):
    heads = q_ref.shape[1] // 128
    k = k_ref[...]
    vt = flip(v_ref[...]).astype(BF)
    vt_ref[...] = vt
    for i in range(kv_ref.shape[0]):
        kv_ref[i, 0] = k
        kv_ref[i, 1] = vt
    for h in range(heads):
        qt_ref[:, h * 128 : (h + 1) * 128] = flip(q_ref[:, h * 128 : (h + 1) * 128]).astype(BF)


def pre_kernel(
    qt_ref, k_ref, vt_ref, wq_ref, wk_ref, fq32_ref, fq_ref, pk_ref, fk_ref, num_ref, den_ref
):
    heads = wq_ref.shape[0] // 64
    k, vt = k_ref[...], vt_ref[...]
    ri = lax.broadcasted_iota(jnp.int32, (128, 128), 0)
    ci = lax.broadcasted_iota(jnp.int32, (128, 128), 1)
    causal = ri <= ci
    hs = range(heads)
    lk = dot_t(wk_ref[...], k)
    lq = [dot(wq_ref[h * 64 : (h + 1) * 64], qt_ref[:, h * 128 : (h + 1) * 128]) for h in hs]
    fq, fk = [], []
    for h in hs:
        a, b = head_rows(h)
        uq, dq = halves(lq[h])
        uk, dk = halves(lk[h * 64 : (h + 1) * 64])
        fq32_ref[a], fq32_ref[b] = uq, dq
        pk_ref[a], pk_ref[b] = uk, dk
        fk32 = jnp.concatenate([uk, dk], axis=0)
        fq.append(jnp.concatenate([uq, dq], axis=0).astype(BF))
        fk.append((fk32.astype(BF), flip(fk32.astype(BF)).astype(BF)))
        fq_ref[h * 128 : (h + 1) * 128] = fq[h]
        fk_ref[h * 128 : (h + 1) * 128] = fk[h][0]
    amat = [jnp.where(causal, dot(fk[h][1], fq[h]), 0.0) for h in hs]
    for h in hs:
        cols = slice(h * 128, (h + 1) * 128)
        num_ref[:, cols] = dot(vt, amat[h].astype(BF))
        den_ref[:, cols] = jnp.broadcast_to(jnp.sum(amat[h], axis=0, keepdims=True), (8, 128))


def load_chunk(kv_ref, lead, first, cb):
    kc = kv_ref[(*lead, pl.ds(first, cb), 0)].reshape(cb * 128, 128)
    vt = jnp.concatenate([kv_ref[(*lead, first + b, 1)] for b in range(cb)], axis=1)
    return kc, vt


def chunk_step(kc, vt, q_refs, wk, m_ref, l_ref, o_ref, st_ref, c1, put, mask=None, keep=None):
    heads = wk.shape[0] // 64
    tiles = []
    at = 0
    for qi, q_ref in enumerate(q_refs):
        step = min(256, q_ref.shape[1])
        for t in range(0, q_ref.shape[1], step):
            tiles.append((qi, q_ref, slice(t, t + step), slice(at, at + step)))
            at += step

    def scores(i):
        return dot(kc, tiles[i][1][:, tiles[i][2]])

    def weigh(i, st):
        qi, _, _, cols = tiles[i]
        if mask is not None:
            ok = mask(qi, st.shape)
            st = jnp.where(ok, st, NEG)
        m_old = m_ref[:, cols]
        m_new = jnp.maximum(m_old, jnp.max(st, axis=0, keepdims=True))
        p = jnp.exp2((st - m_new) * c1)
        if mask is not None:
            p = jnp.where(ok, p, 0.0)
        alpha = jnp.exp2((m_old - m_new) * c1)
        m_ref[:, cols] = m_new
        l_ref[:, cols] = l_ref[:, cols] * alpha + jnp.sum(p, axis=0, keepdims=True)
        return p.astype(BF), alpha

    def collect(i, p, alpha):
        cols = tiles[i][3]
        o_ref[:, cols] = o_ref[:, cols] * alpha + dot(vt, p)

    feats = []
    logits = dot_t(wk, kc)
    nxt = scores(0)
    per = -(-heads // len(tiles))
    for i in range(len(tiles)):
        st = nxt
        if i + 1 < len(tiles):
            nxt = scores(i + 1)
        for h in range(i * per, min(heads, (i + 1) * per)):
            up, down = halves(logits[h * 64 : (h + 1) * 64])
            put(h, up, down)
            feat = jnp.concatenate([up, down], axis=0)
            if keep is not None:
                feat = jnp.where(keep(feat.shape), feat, 0.0)
            feats.append(feat.astype(BF))
        collect(i, *weigh(i, st))
    vext = jnp.concatenate([vt, jnp.ones((EXT, vt.shape[1]), BF)], axis=0)
    st_ref[...] += dot_t(vext, jnp.concatenate(feats, axis=0))


def putter(pk_ref, lead, first, cb):
    def put(h, up, down):
        a, b = head_rows(h)
        for i in range(cb):
            pk_ref[(*lead, first + i, a)] = up[:, i * 128 : (i + 1) * 128]
            pk_ref[(*lead, first + i, b)] = down[:, i * 128 : (i + 1) * 128]

    return put


def own_kernel(c1, cb, idx_ref, qt_ref, qp_ref, wk_ref, kv_ref, m_ref, l_ref, o_ref, st_ref, pk_ref):
    z, c = idx_ref[1], idx_ref[2]
    m_ref[...] = jnp.full(m_ref.shape, NEG, F32)
    l_ref[...] = jnp.zeros(l_ref.shape, F32)
    o_ref[...] = jnp.zeros(o_ref.shape, F32)
    st_ref[...] = jnp.zeros(st_ref.shape, F32)

    def chunk(i, carry):
        first = i * cb
        kc, vt = load_chunk(kv_ref, (), first, cb)

        def mask(qi, shape):
            row = lax.broadcasted_iota(jnp.int32, shape, 0)
            kpos = (2 * (first + row // 128) + c) * 128 + row % 128
            col = lax.broadcasted_iota(jnp.int32, shape, 1)
            qpos = (2 * z + (c if qi == 0 else 1 - c)) * 128 + col % 128
            return kpos <= qpos

        def keep(shape):
            col = lax.broadcasted_iota(jnp.int32, shape, 1)
            return first + col // 128 < z

        put = putter(pk_ref, (), first, cb)
        chunk_step(kc, vt, (qt_ref, qp_ref), wk_ref[...], m_ref, l_ref, o_ref, st_ref, c1, put, mask, keep)
        return carry

    lax.fori_loop(0, z // cb + 1, chunk, 0)


def slice_steps(c1, cb, valid, qt_ref, qp_ref, wk_ref, kv_ref, pk_ref, m_ref, l_ref, o_ref, st_ref):
    per = kv_ref.shape[0] // cb

    def chunk(i, carry):
        first = i * cb
        kc, vt = load_chunk(kv_ref, (), first, cb)
        put = putter(pk_ref, (), first, cb)
        chunk_step(kc, vt, (qt_ref, qp_ref), wk_ref[...], m_ref, l_ref, o_ref, st_ref, c1, put)
        return carry

    lax.fori_loop(0, jnp.where(valid, per, 0), chunk, 0)


def mid_kernel(
    c1, cb, nx, idx_ref, qt_ref, qp_ref, wk_ref, ka_ref, kb_ref, mi_ref, li_ref, oi_ref, si_ref,
    m_ref, l_ref, o_ref, st_ref, pa_ref, pb_ref,
):
    x = idx_ref[0]
    m_ref[...] = mi_ref[...]
    l_ref[...] = li_ref[...]
    o_ref[...] = oi_ref[...]
    st_ref[...] = si_ref[...]
    refs = (m_ref, l_ref, o_ref, st_ref)
    slice_steps(c1, cb, x >= 1, qt_ref, qp_ref, wk_ref, ka_ref, pa_ref, *refs)
    slice_steps(c1, cb, x == nx - 1, qt_ref, qp_ref, wk_ref, kb_ref, pb_ref, *refs)


def end_kernel(
    c1, cb, idx_ref, qt_ref, qp_ref, wk_ref, kc_ref, kd_ref, mi_ref, li_ref, oi_ref, si_ref, fk_ref, vt_ref,
    keep_ref, send_ref, pc_ref, pd_ref, m_ref, l_ref, o_ref, st_ref,
):
    x, c = idx_ref[0], idx_ref[2]
    m_ref[...] = mi_ref[...]
    l_ref[...] = li_ref[...]
    o_ref[...] = oi_ref[...]
    st_ref[...] = si_ref[...]
    refs = (m_ref, l_ref, o_ref, st_ref)
    slice_steps(c1, cb, x >= 2, qt_ref, qp_ref, wk_ref, kc_ref, pc_ref, *refs)
    slice_steps(c1, cb, x >= 2, qt_ref, qp_ref, wk_ref, kd_ref, pd_ref, *refs)
    half = qt_ref.shape[1]
    rows = st_ref.shape[0]
    pad = jnp.zeros((6, half), F32)
    send_ref[0:128] = o_ref[:, half:]
    send_ref[128:136] = jnp.concatenate([m_ref[:, half:], l_ref[:, half:], pad], axis=0)
    vext = jnp.concatenate([vt_ref[...], jnp.ones((EXT, 128), BF)], axis=0)
    own = dot_t(vext, fk_ref[...])
    send_ref[136 : 136 + rows] = st_ref[...] + jnp.where(c == 0, own, 0.0)
    keep_ref[0:128] = o_ref[:, :half]
    keep_ref[128:136] = jnp.concatenate([m_ref[:, :half], l_ref[:, :half], pad], axis=0)
    keep_ref[136 : 136 + rows] = st_ref[...]


def local_kernel(
    c1, mine_ref, got_ref, q_ref, vt_ref, fq32_ref, fq_ref, fk_ref, num_ref, den_ref,
    y_ref, gq_ref, s_ref, dfk_ref, err_ref,
):
    heads = fq_ref.shape[0] // 128
    rows = 128 + EXT
    v = flip(vt_ref[...]).astype(BF)
    ri = lax.broadcasted_iota(jnp.int32, (128, 128), 0)
    ci = lax.broadcasted_iota(jnp.int32, (128, 128), 1)
    causal = ri <= ci
    hs = range(heads)
    col = [slice(h * 128, (h + 1) * 128) for h in hs]
    state = [mine_ref[136 : 136 + rows, col[h]] + got_ref[136 : 136 + rows, col[h]] for h in hs]
    fq = [fq_ref[col[h]] for h in hs]
    prior = [dot(jnp.concatenate(pieces(state[h], 2), axis=1), jnp.concatenate([fq[h], fq[h]], axis=0)) for h in hs]
    t32 = [state[h][0:128].T for h in hs]
    n32 = [jnp.broadcast_to(state[h][128:129], (128, 128)).T for h in hs]
    total = jnp.zeros((128, 128), F32)
    dnum, dden, dnb = [], [], []
    for h in hs:
        ma, la = mine_ref[128:129, col[h]], mine_ref[129:130, col[h]]
        mb, lb = got_ref[128:129, col[h]], got_ref[129:130, col[h]]
        m = jnp.maximum(ma, mb)
        wa, wb = jnp.exp2((ma - m) * c1), jnp.exp2((mb - m) * c1)
        inv_l = 1.0 / (la * wa + lb * wb)
        teacher = mine_ref[0:128, col[h]] * (wa * inv_l) + got_ref[0:128, col[h]] * (wb * inv_l)
        inv = 1.0 / (den_ref[0:1, col[h]] + prior[h][128:129])
        y = (num_ref[:, col[h]] + prior[h][0:128]) * inv
        y_ref[:, col[h]] = y.T.astype(BF)
        diff = y - teacher
        total = total + diff * diff
        dy = 2.0 * diff
        dnum.append(dy * inv)
        dden.append(-jnp.sum(dy * y, axis=0, keepdims=True) * inv)
        dnb.append(dnum[h].astype(BF))
    dmat = [jnp.where(causal, dot(v, dnb[h]) + dden[h], 0.0).astype(BF) for h in hs]
    for h in hs:
        e = jnp.concatenate(pieces(jnp.broadcast_to(dden[h], (128, 128)), 2), axis=1)
        n = dot_t(jnp.concatenate([fq[h], fq[h]], axis=1), e)
        s_ref[0, col[h]] = dot_t(fq[h], dnb[h]).astype(BF)
        s_ref[1, col[h]], s_ref[2, col[h]] = pieces(n, 2)
    for h in hs:
        dfk_ref[col[h]] = dot_t(fq[h], dmat[h])
    dls = []
    for h in hs:
        t1, t2 = pieces(t32[h], 2)
        d1, d2 = pieces(dnum[h], 2)
        left = jnp.concatenate([fk_ref[col[h]], t1, t1, t2], axis=1)
        right = jnp.concatenate([dmat[h], d1, d2, d1], axis=0)
        dfq = dot(left, right) + n32[h] * dden[h]
        a, b = head_rows(h)
        dls.append((half_grad(fq32_ref[a], dfq[0:64]) - half_grad(fq32_ref[b], dfq[64:128])).astype(BF))
    for h in hs:
        gq_ref[h * 64 : (h + 1) * 64] = dot(dls[h], q_ref[:, col[h]])
    err = jnp.sum(jnp.sum(total, axis=0, keepdims=True), axis=1, keepdims=True)
    err_ref[...] = jnp.broadcast_to(err.reshape(1, 1, 1), err_ref.shape)


def later_kernel(
    cb, nx, idx_ref, s_ref, sp_ref, dfk_ref, pown_ref, k_ref, vt_ref, gq_ref, kz_ref, pz_ref,
    ka_ref, pa_ref, kb_ref, pb_ref, kc_ref, pc_ref, kd_ref, pd_ref, err_ref, out_ref, g_ref, w_ref, n_ref,
):
    x, z, c = idx_ref[0], idx_ref[1], idx_ref[2]
    heads = dfk_ref.shape[0] // 128
    w_ref[:, 0:128] = s_ref[0]
    w_ref[:, 128:256] = sp_ref[0]
    n_par = sp_ref[1].astype(F32) + sp_ref[2].astype(F32)
    n_ref[...] = (s_ref[1].astype(F32) + s_ref[2].astype(F32)) + n_par
    vt, k = vt_ref[...], k_ref[...]
    dfk = dfk_ref[...] + jnp.where(c == 0, dot(sp_ref[0], vt) + n_par, 0.0)
    parts = []
    for h in range(heads):
        a, b = head_rows(h)
        parts.append(half_grad(pown_ref[a], dfk[a]) - half_grad(pown_ref[b], dfk[b]))
    g_ref[...] = dot(jnp.concatenate(parts, axis=0).astype(BF), k)

    def term(k_ref, p_ref, lead, first, keep=None):
        kc, vc = load_chunk(k_ref, lead, first, cb)
        v2 = jnp.concatenate([vc, vc], axis=0)
        raw = [dot(w_ref[h * 128 : (h + 1) * 128, :], v2) for h in range(heads)]
        out = []
        for h in range(heads):
            bias = n_ref[h * 128 : (h + 1) * 128]
            d = raw[h] + jnp.concatenate([bias] * cb, axis=1)
            a, b = head_rows(h)
            up = jnp.concatenate([p_ref[(*lead, first + i, a)] for i in range(cb)], axis=1)
            down = jnp.concatenate([p_ref[(*lead, first + i, b)] for i in range(cb)], axis=1)
            out.append(half_grad(up, d[0:64]) - half_grad(down, d[64:128]))
        dl = jnp.concatenate(out, axis=0)
        if keep is not None:
            dl = jnp.where(keep(dl.shape), dl, 0.0)
        g_ref[...] += dot(dl.astype(BF), kc)

    def own_slice(i, carry):
        first = i * cb

        def keep(shape):
            return first + lax.broadcasted_iota(jnp.int32, shape, 1) // 128 < z

        term(kz_ref, pz_ref, (), first, keep)
        return carry

    lax.fori_loop(0, (z + cb - 1) // cb, own_slice, 0)

    def earlier(kx_ref, px_ref, valid):
        def step(i, carry):
            term(kx_ref, px_ref, (), i * cb)
            return carry

        lax.fori_loop(0, jnp.where(valid, kx_ref.shape[0] // cb, 0), step, 0)

    earlier(ka_ref, pa_ref, x >= 1)
    earlier(kb_ref, pb_ref, x == nx - 1)
    earlier(kc_ref, pc_ref, x >= 2)
    earlier(kd_ref, pd_ref, x >= 2)
    e = jnp.sum(err_ref[:, 0, :], axis=0, keepdims=True)
    half = g_ref.shape[0]
    count, width = out_ref.shape[0], out_ref.shape[2]
    per = width // 128 - 1
    for i in range(count):
        for r in range(per):
            row = i * per + r
            src = gq_ref[row : row + 1, :] if row < half else g_ref[row - half : row - half + 1, :]
            out_ref[i, :, r * 128 : (r + 1) * 128] = src
        out_ref[i, :, per * 128 :] = e


def total_kernel(count, in_ref, out_ref, e_ref):
    width = out_ref.shape[2]
    total = jnp.sum(in_ref[...], axis=0)
    out_ref[...] = jnp.broadcast_to(total[None, :, :width], out_ref.shape)
    e_ref[...] = total[:, width:] / count


def body(queries, keys, values, feat_q, feat_k):
    rows = queries.shape[0]
    heads = feat_q.shape[0]
    hd = keys.shape[1]
    nx, nz = lax.axis_size("x"), lax.axis_size("z")
    nh = lax.axis_size("head")
    nctx = nx * nz * 2
    nhalf = nz // 2
    cb = min(4, nhalf)
    idx = jnp.stack([lax.axis_index("x"), lax.axis_index("z"), lax.axis_index("c")]).astype(jnp.int32)
    c1 = hd**-0.5 * LOG2E
    wide = heads * 128
    srows = 128 + EXT

    def swap(a):
        return lax.ppermute(a, "c", [(0, 1), (1, 0)])

    def shift(a, by):
        return lax.ppermute(a, "x", [(i, (i + by) % nx) for i in range(nx)])

    wq = jnp.swapaxes(feat_q, 1, 2).reshape(heads * 64, hd)
    wk = jnp.swapaxes(feat_k, 1, 2).reshape(heads * 64, hd)
    qt, kv, vt = call(
        prep_kernel,
        [((hd, wide), BF), ((nz, 2, 128, 128), BF), ((128, 128), BF)],
        (queries, keys, values),
    )
    kvz = lax.all_to_all(kv, "z", 0, 0, tiled=True)
    ka, kb = shift(kvz, 1), shift(kvz, -1)
    qp = swap(qt)
    fq32, fq, pown, fk, num, den = call(
        pre_kernel,
        [
            ((wide, 128), F32),
            ((wide, 128), BF),
            ((wide, 128), F32),
            ((wide, 128), BF),
            ((128, wide), F32),
            ((8, wide), F32),
        ],
        (qt, keys, vt, wq, wk),
    )
    carry = [
        ((1, 2 * wide), F32),
        ((1, 2 * wide), F32),
        ((hd, 2 * wide), F32),
        ((srows, wide), F32),
    ]
    m, l, o, st, pz = call(
        functools.partial(own_kernel, c1, cb),
        carry + [((nz, wide, 128), F32)],
        (idx, qt, qp, wk, kvz),
        n_smem=1,
    )
    ka, kb, m = lax.optimization_barrier((ka, kb, m))
    kc, kd = shift(ka[:nhalf], 1), shift(kb[nhalf:], -1)
    m, l, o, st, pa, pb = call(
        functools.partial(mid_kernel, c1, cb, nx),
        carry + [((nz, wide, 128), F32)] * 2,
        (idx, qt, qp, wk, ka, kb, m, l, o, st),
        n_smem=1,
    )
    mine, send, pc, pd = call(
        functools.partial(end_kernel, c1, cb),
        [((136 + srows, wide), F32)] * 2 + [((nhalf, wide, 128), F32)] * 2,
        (idx, qt, qp, wk, kc, kd, m, l, o, st, fk, vt),
        n_smem=1,
        scratch=[pltpu.VMEM(s, d) for s, d in carry],
    )
    got = swap(send)
    student, gq, s, dfk, err = call(
        functools.partial(local_kernel, c1),
        [
            ((rows, wide), BF),
            ((heads * 64, 128), F32),
            ((3, wide, 128), BF),
            ((wide, 128), F32),
            ((nh, 8, 128), F32),
        ],
        (mine, got, queries, vt, fq32, fq, fk, num, den),
    )
    sp = swap(s)
    err_h = lax.all_to_all(err, "head", 0, 0, tiled=True)
    share = 2 * heads * 64 * 128 // nctx
    (out,) = call(
        functools.partial(later_kernel, cb, nx),
        [((nctx, 1, share + 128), F32)],
        (idx, s, sp, dfk, pown, keys, vt, gq, kvz, pz, ka, pa, kb, pb, kc, pc, kd, pd, err_h),
        n_smem=1,
        scratch=[
            pltpu.VMEM((heads * 64, 128), F32),
            pltpu.VMEM((wide, 256), BF),
            pltpu.VMEM((wide, 128), F32),
        ],
    )
    arrived = lax.all_to_all(out, CTX, 0, 0, tiled=True)
    final, error = call(
        functools.partial(total_kernel, float(nctx * nh * rows * wide)),
        [((nctx, 1, share), F32), ((1, 128), F32)],
        (arrived,),
    )
    final, error = lax.optimization_barrier((final, error[0, 0]))
    final = lax.all_to_all(final, CTX, 0, 0, tiled=True).reshape(2, heads, 64, 128)
    grads = jnp.swapaxes(final, 2, 3)
    return student, grads[0], grads[1], error


def solution(mesh):
    nctx = mesh.shape["ctx"]
    split = Mesh(
        mesh.devices.reshape(4, nctx // 8, 2, mesh.shape["head"]), ("x", "z", "c", "head")
    )
    in_specs = (
        P(CTX, "head"),
        P(CTX, "head"),
        P(CTX, "head"),
        P("head", None, None),
        P("head", None, None),
    )
    out_specs = (P(CTX, "head"), P("head", None, None), P("head", None, None), P())
    return jax.shard_map(body, mesh=split, in_specs=in_specs, out_specs=out_specs, check_vma=False)
```

```python
import functools

import jax
import jax.numpy as jnp
from jax import lax
from jax.experimental import pallas as pl
from jax.experimental.pallas import tpu as pltpu
from jax.sharding import Mesh
from jax.sharding import PartitionSpec as P

CTX = ("x", "z", "c")
BF = jnp.bfloat16
F32 = jnp.float32
NEG = -1e30
LOG2E = 1.4426950408889634
EXT = 16


def dot(a, b):
    return lax.dot_general(a, b, (((1,), (0,)), ((), ())), preferred_element_type=F32)


def dot_t(a, b):
    return lax.dot_general(a, b, (((1,), (1,)), ((), ())), preferred_element_type=F32)


def flip(a):
    return a.astype(F32).T


def pieces(a, count):
    out = []
    for _ in range(count):
        top = a.astype(BF)
        out.append(top)
        a = a - top.astype(F32)
    return out


def halves(logits):
    high = jnp.max(logits, axis=0, keepdims=True)
    low = jnp.min(logits, axis=0, keepdims=True)
    up = jnp.exp(logits - high)
    down = jnp.exp(low - logits)
    up = up * (1.0 / jnp.sum(up, axis=0, keepdims=True))
    down = down * (1.0 / jnp.sum(down, axis=0, keepdims=True))
    return up, down


def half_grad(p, d):
    return p * (d - jnp.sum(d * p, axis=0, keepdims=True))


def head_rows(h):
    return slice(h * 128, h * 128 + 64), slice(h * 128 + 64, (h + 1) * 128)


def call(kernel, outs, ins, n_smem=0, scratch=(), mib=16, n_hbm=0):
    vm = pl.BlockSpec(memory_space=pltpu.VMEM)
    sm = pl.BlockSpec(memory_space=pltpu.SMEM)
    hbm = pl.BlockSpec(memory_space=pltpu.HBM)
    return pl.pallas_call(
        kernel,
        out_shape=[jax.ShapeDtypeStruct(s, d) for s, d in outs],
        in_specs=[sm] * n_smem + [hbm] * n_hbm + [vm] * (len(ins) - n_smem - n_hbm),
        out_specs=[vm] * len(outs),
        scratch_shapes=list(scratch),
        compiler_params=pltpu.CompilerParams(vmem_limit_bytes=mib * 1024 * 1024),
    )(*ins)


def prep_kernel(q_hbm, k_hbm, v_hbm, qt_ref, kv_ref, vt_ref, q_ref, k_ref, v_ref, sems):
    heads = q_ref.shape[1] // 128
    copies = [
        pltpu.make_async_copy(src, dst, sems.at[i])
        for i, (src, dst) in enumerate(((k_hbm, k_ref), (v_hbm, v_ref), (q_hbm, q_ref)))
    ]
    for copy in copies:
        copy.start()
    copies[0].wait()
    copies[1].wait()
    k = k_ref[...]
    vt = flip(v_ref[...]).astype(BF)
    vt_ref[...] = vt
    for i in range(kv_ref.shape[0]):
        kv_ref[i, 0] = k
        kv_ref[i, 1] = vt
    copies[2].wait()
    for h in range(heads):
        qt_ref[:, h * 128 : (h + 1) * 128] = flip(q_ref[:, h * 128 : (h + 1) * 128]).astype(BF)


def pre_kernel(
    qt_ref, k_ref, vt_ref, wq_ref, wk_ref, fq32_ref, fq_ref, pk_ref, fk_ref, num_ref, den_ref
):
    heads = wq_ref.shape[0] // 64
    k, vt = k_ref[...], vt_ref[...]
    ri = lax.broadcasted_iota(jnp.int32, (128, 128), 0)
    ci = lax.broadcasted_iota(jnp.int32, (128, 128), 1)
    causal = ri <= ci
    hs = range(heads)
    lk = dot_t(wk_ref[...], k)
    lq = [dot(wq_ref[h * 64 : (h + 1) * 64], qt_ref[:, h * 128 : (h + 1) * 128]) for h in hs]
    fq, fk = [], []
    for h in hs:
        a, b = head_rows(h)
        uq, dq = halves(lq[h])
        uk, dk = halves(lk[h * 64 : (h + 1) * 64])
        fq32_ref[a], fq32_ref[b] = uq, dq
        pk_ref[a], pk_ref[b] = uk, dk
        fk32 = jnp.concatenate([uk, dk], axis=0)
        fq.append(jnp.concatenate([uq, dq], axis=0).astype(BF))
        fk.append((fk32.astype(BF), flip(fk32.astype(BF)).astype(BF)))
        fq_ref[h * 128 : (h + 1) * 128] = fq[h]
        fk_ref[h * 128 : (h + 1) * 128] = fk[h][0]
    amat = [jnp.where(causal, dot(fk[h][1], fq[h]), 0.0) for h in hs]
    for h in hs:
        cols = slice(h * 128, (h + 1) * 128)
        num_ref[:, cols] = dot(vt, amat[h].astype(BF))
        den_ref[:, cols] = jnp.broadcast_to(jnp.sum(amat[h], axis=0, keepdims=True), (8, 128))


def load_chunk(kv_ref, lead, first, cb):
    kc = kv_ref[(*lead, pl.ds(first, cb), 0)].reshape(cb * 128, 128)
    vt = jnp.concatenate([kv_ref[(*lead, first + b, 1)] for b in range(cb)], axis=1)
    return kc, vt


def chunk_step(kc, vt, q_refs, wk, m_ref, l_ref, o_ref, st_ref, c1, put, mask=None, keep=None):
    heads = wk.shape[0] // 64
    tiles = []
    at = 0
    for qi, q_ref in enumerate(q_refs):
        step = min(256, q_ref.shape[1])
        for t in range(0, q_ref.shape[1], step):
            tiles.append((qi, q_ref, slice(t, t + step), slice(at, at + step)))
            at += step

    def scores(i):
        return dot(kc, tiles[i][1][:, tiles[i][2]])

    def weigh(i, st):
        qi, _, _, cols = tiles[i]
        if mask is not None:
            ok = mask(qi, st.shape)
            st = jnp.where(ok, st, NEG)
        m_old = m_ref[:, cols]
        m_new = jnp.maximum(m_old, jnp.max(st, axis=0, keepdims=True))
        p = jnp.exp2((st - m_new) * c1)
        if mask is not None:
            p = jnp.where(ok, p, 0.0)
        alpha = jnp.exp2((m_old - m_new) * c1)
        m_ref[:, cols] = m_new
        l_ref[:, cols] = l_ref[:, cols] * alpha + jnp.sum(p, axis=0, keepdims=True)
        return p.astype(BF), alpha

    def collect(i, p, alpha):
        cols = tiles[i][3]
        o_ref[:, cols] = o_ref[:, cols] * alpha + dot(vt, p)

    feats = []
    logits = dot_t(wk, kc)
    nxt = scores(0)
    per = -(-heads // len(tiles))
    for i in range(len(tiles)):
        st = nxt
        if i + 1 < len(tiles):
            nxt = scores(i + 1)
        for h in range(i * per, min(heads, (i + 1) * per)):
            up, down = halves(logits[h * 64 : (h + 1) * 64])
            put(h, up, down)
            feat = jnp.concatenate([up, down], axis=0)
            if keep is not None:
                feat = jnp.where(keep(feat.shape), feat, 0.0)
            feats.append(feat.astype(BF))
        collect(i, *weigh(i, st))
    vext = jnp.concatenate([vt, jnp.ones((EXT, vt.shape[1]), BF)], axis=0)
    st_ref[...] += dot_t(vext, jnp.concatenate(feats, axis=0))


def columns_of(idx_ref, qq_ref):
    c = idx_ref[2]
    return qq_ref.at[c], qq_ref.at[1 - c]


def putter(pk_ref, lead, first, cb):
    def put(h, up, down):
        a, b = head_rows(h)
        for i in range(cb):
            pk_ref[(*lead, first + i, a)] = up[:, i * 128 : (i + 1) * 128]
            pk_ref[(*lead, first + i, b)] = down[:, i * 128 : (i + 1) * 128]

    return put


def own_kernel(c1, cb, idx_ref, qq_ref, wk_ref, kv_ref, m_ref, l_ref, o_ref, st_ref, pk_ref):
    z, c = idx_ref[1], idx_ref[2]
    m_ref[...] = jnp.full(m_ref.shape, NEG, F32)
    l_ref[...] = jnp.zeros(l_ref.shape, F32)
    o_ref[...] = jnp.zeros(o_ref.shape, F32)
    st_ref[...] = jnp.zeros(st_ref.shape, F32)

    def chunk(i, carry):
        first = i * cb
        kc, vt = load_chunk(kv_ref, (), first, cb)

        def mask(qi, shape):
            row = lax.broadcasted_iota(jnp.int32, shape, 0)
            kpos = (2 * (first + row // 128) + c) * 128 + row % 128
            col = lax.broadcasted_iota(jnp.int32, shape, 1)
            qpos = (2 * z + (c if qi == 0 else 1 - c)) * 128 + col % 128
            return kpos <= qpos

        def keep(shape):
            col = lax.broadcasted_iota(jnp.int32, shape, 1)
            return first + col // 128 < z

        put = putter(pk_ref, (), first, cb)
        chunk_step(kc, vt, columns_of(idx_ref, qq_ref), wk_ref[...], m_ref, l_ref, o_ref, st_ref, c1, put, mask, keep)
        return carry

    lax.fori_loop(0, z // cb + 1, chunk, 0)


def slice_steps(c1, cb, valid, idx_ref, qq_ref, wk_ref, kv_ref, pk_ref, m_ref, l_ref, o_ref, st_ref):
    per = kv_ref.shape[0] // cb

    def chunk(i, carry):
        first = i * cb
        kc, vt = load_chunk(kv_ref, (), first, cb)
        put = putter(pk_ref, (), first, cb)
        chunk_step(kc, vt, columns_of(idx_ref, qq_ref), wk_ref[...], m_ref, l_ref, o_ref, st_ref, c1, put)
        return carry

    lax.fori_loop(0, jnp.where(valid, per, 0), chunk, 0)


def mid_kernel(
    c1, cb, nx, idx_ref, qq_ref, wk_ref, ka_ref, kb_ref, mi_ref, li_ref, oi_ref, si_ref,
    m_ref, l_ref, o_ref, st_ref, pa_ref, pb_ref,
):
    x = idx_ref[0]
    m_ref[...] = mi_ref[...]
    l_ref[...] = li_ref[...]
    o_ref[...] = oi_ref[...]
    st_ref[...] = si_ref[...]
    refs = (m_ref, l_ref, o_ref, st_ref)
    slice_steps(c1, cb, x >= 1, idx_ref, qq_ref, wk_ref, ka_ref, pa_ref, *refs)
    slice_steps(c1, cb, x == nx - 1, idx_ref, qq_ref, wk_ref, kb_ref, pb_ref, *refs)


def end_kernel(
    c1, cb, idx_ref, qq_ref, wk_ref, kc_ref, kd_ref, mi_ref, li_ref, oi_ref, si_ref, fk_ref, vt_ref,
    keep_ref, send_ref, pc_ref, pd_ref, m_ref, l_ref, o_ref, st_ref,
):
    x, c = idx_ref[0], idx_ref[2]
    m_ref[...] = mi_ref[...]
    l_ref[...] = li_ref[...]
    o_ref[...] = oi_ref[...]
    st_ref[...] = si_ref[...]
    refs = (m_ref, l_ref, o_ref, st_ref)
    slice_steps(c1, cb, x >= 2, idx_ref, qq_ref, wk_ref, kc_ref, pc_ref, *refs)
    slice_steps(c1, cb, x >= 2, idx_ref, qq_ref, wk_ref, kd_ref, pd_ref, *refs)
    half = qq_ref.shape[2]
    rows = st_ref.shape[0]
    pad = jnp.zeros((6, half), F32)
    send_ref[0:128] = o_ref[:, half:]
    send_ref[128:136] = jnp.concatenate([m_ref[:, half:], l_ref[:, half:], pad], axis=0)
    vext = jnp.concatenate([vt_ref[...], jnp.ones((EXT, 128), BF)], axis=0)
    own = dot_t(vext, fk_ref[...])
    send_ref[136 : 136 + rows] = st_ref[...] + jnp.where(c == 0, own, 0.0)
    keep_ref[0:128] = o_ref[:, :half]
    keep_ref[128:136] = jnp.concatenate([m_ref[:, :half], l_ref[:, :half], pad], axis=0)
    keep_ref[136 : 136 + rows] = st_ref[...]


def local_kernel(
    c1, mine_ref, got_ref, q_ref, vt_ref, fq32_ref, fq_ref, fk_ref, num_ref, den_ref,
    y_ref, gq_ref, s_ref, dfk_ref, err_ref,
):
    heads = fq_ref.shape[0] // 128
    rows = 128 + EXT
    v = flip(vt_ref[...]).astype(BF)
    ri = lax.broadcasted_iota(jnp.int32, (128, 128), 0)
    ci = lax.broadcasted_iota(jnp.int32, (128, 128), 1)
    causal = ri <= ci
    hs = range(heads)
    col = [slice(h * 128, (h + 1) * 128) for h in hs]
    state = [mine_ref[136 : 136 + rows, col[h]] + got_ref[136 : 136 + rows, col[h]] for h in hs]
    fq = [fq_ref[col[h]] for h in hs]
    prior = [dot(jnp.concatenate(pieces(state[h], 2), axis=1), jnp.concatenate([fq[h], fq[h]], axis=0)) for h in hs]
    t32 = [state[h][0:128].T for h in hs]
    n32 = [jnp.broadcast_to(state[h][128:129], (128, 128)).T for h in hs]
    total = jnp.zeros((128, 128), F32)
    dnum, dden, dnb = [], [], []
    for h in hs:
        ma, la = mine_ref[128:129, col[h]], mine_ref[129:130, col[h]]
        mb, lb = got_ref[128:129, col[h]], got_ref[129:130, col[h]]
        m = jnp.maximum(ma, mb)
        wa, wb = jnp.exp2((ma - m) * c1), jnp.exp2((mb - m) * c1)
        inv_l = 1.0 / (la * wa + lb * wb)
        teacher = mine_ref[0:128, col[h]] * (wa * inv_l) + got_ref[0:128, col[h]] * (wb * inv_l)
        inv = 1.0 / (den_ref[0:1, col[h]] + prior[h][128:129])
        y = (num_ref[:, col[h]] + prior[h][0:128]) * inv
        y_ref[:, col[h]] = y.T.astype(BF)
        diff = y - teacher
        total = total + diff * diff
        dy = 2.0 * diff
        dnum.append(dy * inv)
        dden.append(-jnp.sum(dy * y, axis=0, keepdims=True) * inv)
        dnb.append(dnum[h].astype(BF))
    dmat = [jnp.where(causal, dot(v, dnb[h]) + dden[h], 0.0).astype(BF) for h in hs]
    for h in hs:
        e = jnp.concatenate(pieces(jnp.broadcast_to(dden[h], (128, 128)), 2), axis=1)
        n = dot_t(jnp.concatenate([fq[h], fq[h]], axis=1), e)
        s_ref[0, col[h]] = dot_t(fq[h], dnb[h]).astype(BF)
        s_ref[1, col[h]], s_ref[2, col[h]] = pieces(n, 2)
    for h in hs:
        dfk_ref[col[h]] = dot_t(fq[h], dmat[h])
    dls = []
    for h in hs:
        t1, t2 = pieces(t32[h], 2)
        d1, d2 = pieces(dnum[h], 2)
        left = jnp.concatenate([fk_ref[col[h]], t1, t1, t2], axis=1)
        right = jnp.concatenate([dmat[h], d1, d2, d1], axis=0)
        dfq = dot(left, right) + n32[h] * dden[h]
        a, b = head_rows(h)
        dls.append((half_grad(fq32_ref[a], dfq[0:64]) - half_grad(fq32_ref[b], dfq[64:128])).astype(BF))
    for h in hs:
        gq_ref[h * 64 : (h + 1) * 64] = dot(dls[h], q_ref[:, col[h]])
    err = jnp.sum(jnp.sum(total, axis=0, keepdims=True), axis=1, keepdims=True)
    err_ref[...] = jnp.broadcast_to(err, err_ref.shape)


def later_kernel(
    cb, nx, idx_ref, s_ref, sp_ref, dfk_ref, pown_ref, k_ref, vt_ref, gq_ref, kz_ref, pz_ref,
    ka_ref, pa_ref, kb_ref, pb_ref, kc_ref, pc_ref, kd_ref, pd_ref, e_ref, r_ref, out_ref, esum_ref, g_ref, w_ref, n_ref,
):
    x, z, c = idx_ref[0], idx_ref[1], idx_ref[2]
    heads = dfk_ref.shape[0] // 128
    w_ref[:, 0:128] = s_ref[0]
    w_ref[:, 128:256] = sp_ref[0]
    n_par = sp_ref[1].astype(F32) + sp_ref[2].astype(F32)
    n_ref[...] = (s_ref[1].astype(F32) + s_ref[2].astype(F32)) + n_par
    vt, k = vt_ref[...], k_ref[...]
    dfk = dfk_ref[...] + jnp.where(c == 0, dot(sp_ref[0], vt) + n_par, 0.0)
    parts = []
    for h in range(heads):
        a, b = head_rows(h)
        parts.append(half_grad(pown_ref[a], dfk[a]) - half_grad(pown_ref[b], dfk[b]))
    g_ref[...] = dot(jnp.concatenate(parts, axis=0).astype(BF), k)

    def term(k_ref, p_ref, lead, first, keep=None):
        kc, vc = load_chunk(k_ref, lead, first, cb)
        v2 = jnp.concatenate([vc, vc], axis=0)
        raw = [dot(w_ref[h * 128 : (h + 1) * 128, :], v2) for h in range(heads)]
        out = []
        for h in range(heads):
            bias = n_ref[h * 128 : (h + 1) * 128]
            d = raw[h] + jnp.concatenate([bias] * cb, axis=1)
            a, b = head_rows(h)
            up = jnp.concatenate([p_ref[(*lead, first + i, a)] for i in range(cb)], axis=1)
            down = jnp.concatenate([p_ref[(*lead, first + i, b)] for i in range(cb)], axis=1)
            out.append(half_grad(up, d[0:64]) - half_grad(down, d[64:128]))
        dl = jnp.concatenate(out, axis=0)
        if keep is not None:
            dl = jnp.where(keep(dl.shape), dl, 0.0)
        g_ref[...] += dot(dl.astype(BF), kc)

    def own_slice(i, carry):
        first = i * cb

        def keep(shape):
            return first + lax.broadcasted_iota(jnp.int32, shape, 1) // 128 < z

        term(kz_ref, pz_ref, (), first, keep)
        return carry

    lax.fori_loop(0, (z + cb - 1) // cb, own_slice, 0)

    def earlier(kx_ref, px_ref, valid):
        def step(i, carry):
            term(kx_ref, px_ref, (), i * cb)
            return carry

        lax.fori_loop(0, jnp.where(valid, kx_ref.shape[0] // cb, 0), step, 0)

    earlier(ka_ref, pa_ref, x >= 1)
    earlier(kb_ref, pb_ref, x == nx - 1)
    earlier(kc_ref, pc_ref, x >= 2)
    earlier(kd_ref, pd_ref, x >= 2)
    esum_ref[...] = e_ref[...] + r_ref[...]
    half = g_ref.shape[0]
    out_ref[0:half] = gq_ref[...].astype(BF)
    out_ref[half : 2 * half] = g_ref[...].astype(BF)


def total_kernel(in_ref, e_ref, r_ref, out_ref):
    total = jnp.sum(in_ref[...].astype(F32), axis=0)
    parts = [total[r : r + 1] for r in range(total.shape[0])] + [e_ref[0:1] + r_ref[0:1]]
    row = jnp.concatenate(parts, axis=1)
    out_ref[...] = jnp.broadcast_to(row[None], out_ref.shape)


def last_kernel(count, in_ref, gq_ref, gk_ref, e_ref):
    members, width = in_ref.shape[0], in_ref.shape[2]
    per = width // 128 - 1
    half = members // 2
    for i in range(members):
        dst, at = (gq_ref, i) if i < half else (gk_ref, i - half)
        for r in range(per):
            dst[at * per + r : at * per + r + 1, :] = in_ref[i, :, r * 128 : (r + 1) * 128]
    e_ref[...] = jnp.sum(in_ref[:, :, per * 128 :], axis=0) / count


def body(queries, keys, values, feat_q, feat_k):
    rows = queries.shape[0]
    heads = feat_q.shape[0]
    hd = keys.shape[1]
    nx, nz = lax.axis_size("x"), lax.axis_size("z")
    nh = lax.axis_size("head")
    nctx = nx * nz * 2
    nhalf = nz // 2
    cb = min(4, nhalf)
    idx = jnp.stack([lax.axis_index("x"), lax.axis_index("z"), lax.axis_index("c")]).astype(jnp.int32)
    c1 = hd**-0.5 * LOG2E
    wide = heads * 128
    srows = 128 + EXT

    def swap(a):
        return lax.ppermute(a, "c", [(0, 1), (1, 0)])

    def move(a, pairs):
        return lax.ppermute(a, "x", pairs)

    wq = jnp.swapaxes(feat_q, 1, 2).reshape(heads * 64, hd)
    wk = jnp.swapaxes(feat_k, 1, 2).reshape(heads * 64, hd)
    qt, kv, vt = call(
        prep_kernel,
        [((hd, wide), BF), ((nz, 2, 128, 128), BF), ((128, 128), BF)],
        (queries, keys, values),
        n_hbm=3,
        scratch=[
            pltpu.VMEM((rows, wide), BF),
            pltpu.VMEM((rows, hd), BF),
            pltpu.VMEM((rows, hd), BF),
            pltpu.SemaphoreType.DMA((3,)),
        ],
    )
    kvz = lax.all_to_all(kv, "z", 0, 0, tiled=True)
    ka, kb = move(kvz, [(0, 1), (1, 2), (2, 3)]), move(kvz, [(0, 3), (1, 0)])
    both = lax.all_gather(qt, "c")
    fq32, fq, pown, fk, num, den = call(
        pre_kernel,
        [
            ((wide, 128), F32),
            ((wide, 128), BF),
            ((wide, 128), F32),
            ((wide, 128), BF),
            ((128, wide), F32),
            ((8, wide), F32),
        ],
        (qt, keys, vt, wq, wk),
    )
    carry = [
        ((1, 2 * wide), F32),
        ((1, 2 * wide), F32),
        ((hd, 2 * wide), F32),
        ((srows, wide), F32),
    ]
    m, l, o, st, pz = call(
        functools.partial(own_kernel, c1, cb),
        carry + [((nz, wide, 128), F32)],
        (idx, both, wk, kvz),
        n_smem=1,
    )
    ka, kb, m = lax.optimization_barrier((ka, kb, m))
    kc, kd = move(ka[:nhalf], [(1, 2), (2, 3)]), move(kb[nhalf:], [(3, 2), (0, 3)])
    m, l, o, st, pa, pb = call(
        functools.partial(mid_kernel, c1, cb, nx),
        carry + [((nz, wide, 128), F32)] * 2,
        (idx, both, wk, ka, kb, m, l, o, st),
        n_smem=1,
    )
    mine, send, pc, pd = call(
        functools.partial(end_kernel, c1, cb),
        [((136 + srows, wide), F32)] * 2 + [((nhalf, wide, 128), F32)] * 2,
        (idx, both, wk, kc, kd, m, l, o, st, fk, vt),
        n_smem=1,
        scratch=[pltpu.VMEM(s, d) for s, d in carry],
    )
    got = swap(send)
    student, gq, s, dfk, err = call(
        functools.partial(local_kernel, c1),
        [
            ((rows, wide), BF),
            ((heads * 64, 128), F32),
            ((3, wide, 128), BF),
            ((wide, 128), F32),
            ((8, 128), F32),
        ],
        (mine, got, queries, vt, fq32, fq, fk, num, den),
    )
    sp = swap(s)
    steps = [b for b in (1, 2, 4) if b < nh]
    flip_head = lambda a, by: lax.ppermute(a, "head", [(i, i ^ by) for i in range(nh)])
    got_err = flip_head(err, steps[0]) if steps else jnp.zeros_like(err)
    share = 2 * heads * 64 * 128 // nctx
    out, err = call(
        functools.partial(later_kernel, cb, nx),
        [((2 * heads * 64, 128), BF), ((8, 128), F32)],
        (idx, s, sp, dfk, pown, keys, vt, gq, kvz, pz, ka, pa, kb, pb, kc, pc, kd, pd, err, got_err),
        n_smem=1,
        scratch=[
            pltpu.VMEM((heads * 64, 128), F32),
            pltpu.VMEM((wide, 256), BF),
            pltpu.VMEM((wide, 128), F32),
        ],
    )
    got_err = jnp.zeros_like(err)
    for by in steps[1:]:
        err = err + got_err
        got_err = flip_head(err, by)
    arrived = lax.all_to_all(out.reshape(nctx, share // 128, 128), CTX, 0, 0, tiled=True)
    (final,) = call(total_kernel, [((nctx, 1, share + 128), F32)], (arrived, err, got_err))
    final = lax.all_to_all(final, CTX, 0, 0, tiled=True)
    gq, gk, error = call(
        functools.partial(last_kernel, float(nctx * nh * rows * wide)),
        [((heads * 64, 128), F32)] * 2 + [((1, 128), F32)],
        (final,),
    )
    gq, gk = (jnp.swapaxes(g.reshape(heads, 64, 128), 1, 2) for g in (gq, gk))
    return student, gq, gk, error[0, 0]


def solution(mesh):
    nctx = mesh.shape["ctx"]
    split = Mesh(
        mesh.devices.reshape(4, nctx // 8, 2, mesh.shape["head"]), ("x", "z", "c", "head")
    )
    in_specs = (
        P(CTX, "head"),
        P(CTX, "head"),
        P(CTX, "head"),
        P("head", None, None),
        P("head", None, None),
    )
    out_specs = (P(CTX, "head"), P("head", None, None), P("head", None, None), P())
    return jax.shard_map(body, mesh=split, in_specs=in_specs, out_specs=out_specs, check_vma=False)
```

```python
import functools

import jax
import jax.numpy as jnp
from jax import lax
from jax.experimental import pallas as pl
from jax.experimental.pallas import tpu as pltpu
from jax.sharding import Mesh
from jax.sharding import PartitionSpec as P

CTX = ("x", "z", "c")
BF = jnp.bfloat16
F32 = jnp.float32
NEG = -1e30
LOG2E = 1.4426950408889634
EXT = 16


def dot(a, b):
    return lax.dot_general(a, b, (((1,), (0,)), ((), ())), preferred_element_type=F32)


def dot_t(a, b):
    return lax.dot_general(a, b, (((1,), (1,)), ((), ())), preferred_element_type=F32)


def flip(a):
    return a.astype(F32).T


def pieces(a, count):
    out = []
    for _ in range(count):
        top = a.astype(BF)
        out.append(top)
        a = a - top.astype(F32)
    return out


def halves(logits):
    high = jnp.max(logits, axis=0, keepdims=True)
    low = jnp.min(logits, axis=0, keepdims=True)
    up = jnp.exp(logits - high)
    down = jnp.exp(low - logits)
    up = up * (1.0 / jnp.sum(up, axis=0, keepdims=True))
    down = down * (1.0 / jnp.sum(down, axis=0, keepdims=True))
    return up, down


def half_grad(p, d):
    return p * (d - jnp.sum(d * p, axis=0, keepdims=True))


def head_rows(h):
    return slice(h * 128, h * 128 + 64), slice(h * 128 + 64, (h + 1) * 128)


def call(kernel, outs, ins, n_smem=0, scratch=(), mib=16, n_hbm=0):
    vm = pl.BlockSpec(memory_space=pltpu.VMEM)
    sm = pl.BlockSpec(memory_space=pltpu.SMEM)
    hbm = pl.BlockSpec(memory_space=pltpu.HBM)
    return pl.pallas_call(
        kernel,
        out_shape=[jax.ShapeDtypeStruct(s, d) for s, d in outs],
        in_specs=[sm] * n_smem + [hbm] * n_hbm + [vm] * (len(ins) - n_smem - n_hbm),
        out_specs=[vm] * len(outs),
        scratch_shapes=list(scratch),
        compiler_params=pltpu.CompilerParams(vmem_limit_bytes=mib * 1024 * 1024),
    )(*ins)


def prep_kernel(q_hbm, k_hbm, v_hbm, qt_ref, kv_ref, vt_ref, q_ref, k_ref, v_ref, sems):
    heads = q_ref.shape[1] // 128
    copies = [
        pltpu.make_async_copy(src, dst, sems.at[i])
        for i, (src, dst) in enumerate(((k_hbm, k_ref), (v_hbm, v_ref), (q_hbm, q_ref)))
    ]
    for copy in copies:
        copy.start()
    copies[0].wait()
    copies[1].wait()
    k = k_ref[...]
    vt = flip(v_ref[...]).astype(BF)
    vt_ref[...] = vt
    for i in range(kv_ref.shape[0]):
        kv_ref[i, 0] = k
        kv_ref[i, 1] = vt
    copies[2].wait()
    for h in range(heads):
        qt_ref[:, h * 128 : (h + 1) * 128] = flip(q_ref[:, h * 128 : (h + 1) * 128]).astype(BF)


def pre_kernel(
    qt_ref, k_ref, vt_ref, wq_ref, wk_ref, fq32_ref, fq_ref, pk_ref, fk_ref, num_ref, den_ref
):
    heads = wq_ref.shape[0] // 64
    k, vt = k_ref[...], vt_ref[...]
    ri = lax.broadcasted_iota(jnp.int32, (128, 128), 0)
    ci = lax.broadcasted_iota(jnp.int32, (128, 128), 1)
    causal = ri <= ci
    hs = range(heads)
    lk = dot_t(wk_ref[...], k)
    lq = [dot(wq_ref[h * 64 : (h + 1) * 64], qt_ref[:, h * 128 : (h + 1) * 128]) for h in hs]
    fq, fk = [], []
    for h in hs:
        a, b = head_rows(h)
        uq, dq = halves(lq[h])
        uk, dk = halves(lk[h * 64 : (h + 1) * 64])
        fq32_ref[a], fq32_ref[b] = uq, dq
        pk_ref[a], pk_ref[b] = uk, dk
        fk32 = jnp.concatenate([uk, dk], axis=0)
        fq.append(jnp.concatenate([uq, dq], axis=0).astype(BF))
        fk.append((fk32.astype(BF), flip(fk32.astype(BF)).astype(BF)))
        fq_ref[h * 128 : (h + 1) * 128] = fq[h]
        fk_ref[h * 128 : (h + 1) * 128] = fk[h][0]
    amat = [jnp.where(causal, dot(fk[h][1], fq[h]), 0.0) for h in hs]
    for h in hs:
        cols = slice(h * 128, (h + 1) * 128)
        num_ref[:, cols] = dot(vt, amat[h].astype(BF))
        den_ref[:, cols] = jnp.broadcast_to(jnp.sum(amat[h], axis=0, keepdims=True), (8, 128))


def load_chunk(kv_ref, lead, first, cb):
    kc = kv_ref[(*lead, pl.ds(first, cb), 0)].reshape(cb * 128, 128)
    vt = jnp.concatenate([kv_ref[(*lead, first + b, 1)] for b in range(cb)], axis=1)
    return kc, vt


def chunk_step(kc, vt, q_refs, wk, m_ref, l_ref, o_ref, st_ref, c1, put, mask=None, keep=None):
    heads = wk.shape[0] // 64
    tiles = []
    at = 0
    for qi, q_ref in enumerate(q_refs):
        step = min(256, q_ref.shape[1])
        for t in range(0, q_ref.shape[1], step):
            tiles.append((qi, q_ref, slice(t, t + step), slice(at, at + step)))
            at += step

    def scores(i):
        return dot(kc, tiles[i][1][:, tiles[i][2]])

    def weigh(i, st):
        qi, _, _, cols = tiles[i]
        if mask is not None:
            ok = mask(qi, st.shape)
            st = jnp.where(ok, st, NEG)
        m_old = m_ref[:, cols]
        m_new = jnp.maximum(m_old, jnp.max(st, axis=0, keepdims=True))
        p = jnp.exp2((st - m_new) * c1)
        if mask is not None:
            p = jnp.where(ok, p, 0.0)
        alpha = jnp.exp2((m_old - m_new) * c1)
        m_ref[:, cols] = m_new
        l_ref[:, cols] = l_ref[:, cols] * alpha + jnp.sum(p, axis=0, keepdims=True)
        return p.astype(BF), alpha

    def collect(i, p, alpha):
        cols = tiles[i][3]
        o_ref[:, cols] = o_ref[:, cols] * alpha + dot(vt, p)

    feats = []
    logits = dot_t(wk, kc)
    nxt = scores(0)
    per = -(-heads // len(tiles))
    for i in range(len(tiles)):
        st = nxt
        if i + 1 < len(tiles):
            nxt = scores(i + 1)
        for h in range(i * per, min(heads, (i + 1) * per)):
            up, down = halves(logits[h * 64 : (h + 1) * 64])
            put(h, up, down)
            feat = jnp.concatenate([up, down], axis=0)
            if keep is not None:
                feat = jnp.where(keep(feat.shape), feat, 0.0)
            feats.append(feat.astype(BF))
        collect(i, *weigh(i, st))
    vext = jnp.concatenate([vt, jnp.ones((EXT, vt.shape[1]), BF)], axis=0)
    st_ref[...] += dot_t(vext, jnp.concatenate(feats, axis=0))


def columns_of(idx_ref, qq_ref):
    c = idx_ref[2]
    return qq_ref.at[c], qq_ref.at[1 - c]


def putter(pk_ref, lead, first, cb):
    def put(h, up, down):
        a, b = head_rows(h)
        for i in range(cb):
            pk_ref[(*lead, first + i, a)] = up[:, i * 128 : (i + 1) * 128]
            pk_ref[(*lead, first + i, b)] = down[:, i * 128 : (i + 1) * 128]

    return put


def own_kernel(c1, cb, idx_ref, qq_ref, wk_ref, kv_ref, m_ref, l_ref, o_ref, st_ref, pk_ref):
    z, c = idx_ref[1], idx_ref[2]
    m_ref[...] = jnp.full(m_ref.shape, NEG, F32)
    l_ref[...] = jnp.zeros(l_ref.shape, F32)
    o_ref[...] = jnp.zeros(o_ref.shape, F32)
    st_ref[...] = jnp.zeros(st_ref.shape, F32)

    def chunk(i, carry):
        first = i * cb
        kc, vt = load_chunk(kv_ref, (), first, cb)

        def mask(qi, shape):
            row = lax.broadcasted_iota(jnp.int32, shape, 0)
            kpos = (2 * (first + row // 128) + c) * 128 + row % 128
            col = lax.broadcasted_iota(jnp.int32, shape, 1)
            qpos = (2 * z + (c if qi == 0 else 1 - c)) * 128 + col % 128
            return kpos <= qpos

        def keep(shape):
            col = lax.broadcasted_iota(jnp.int32, shape, 1)
            return first + col // 128 < z

        put = putter(pk_ref, (), first, cb)
        chunk_step(kc, vt, columns_of(idx_ref, qq_ref), wk_ref[...], m_ref, l_ref, o_ref, st_ref, c1, put, mask, keep)
        return carry

    lax.fori_loop(0, z // cb + 1, chunk, 0)


def slice_steps(c1, cb, valid, idx_ref, qq_ref, wk_ref, kv_ref, pk_ref, m_ref, l_ref, o_ref, st_ref):
    per = kv_ref.shape[0] // cb

    def chunk(i, carry):
        first = i * cb
        kc, vt = load_chunk(kv_ref, (), first, cb)
        put = putter(pk_ref, (), first, cb)
        chunk_step(kc, vt, columns_of(idx_ref, qq_ref), wk_ref[...], m_ref, l_ref, o_ref, st_ref, c1, put)
        return carry

    lax.fori_loop(0, jnp.where(valid, per, 0), chunk, 0)


def mid_kernel(
    c1, cb, nx, idx_ref, qq_ref, wk_ref, ka_ref, kb_ref, mi_ref, li_ref, oi_ref, si_ref,
    m_ref, l_ref, o_ref, st_ref, pa_ref, pb_ref,
):
    x = idx_ref[0]
    m_ref[...] = mi_ref[...]
    l_ref[...] = li_ref[...]
    o_ref[...] = oi_ref[...]
    st_ref[...] = si_ref[...]
    refs = (m_ref, l_ref, o_ref, st_ref)
    slice_steps(c1, cb, x >= 1, idx_ref, qq_ref, wk_ref, ka_ref, pa_ref, *refs)
    slice_steps(c1, cb, x == nx - 1, idx_ref, qq_ref, wk_ref, kb_ref, pb_ref, *refs)


def end_kernel(
    c1, cb, idx_ref, qq_ref, wk_ref, kc_ref, kd_ref, mi_ref, li_ref, oi_ref, si_ref, fk_ref, vt_ref,
    keep_ref, send_ref, pc_ref, pd_ref, m_ref, l_ref, o_ref, st_ref,
):
    x, c = idx_ref[0], idx_ref[2]
    m_ref[...] = mi_ref[...]
    l_ref[...] = li_ref[...]
    o_ref[...] = oi_ref[...]
    st_ref[...] = si_ref[...]
    refs = (m_ref, l_ref, o_ref, st_ref)
    slice_steps(c1, cb, x >= 2, idx_ref, qq_ref, wk_ref, kc_ref, pc_ref, *refs)
    slice_steps(c1, cb, x >= 2, idx_ref, qq_ref, wk_ref, kd_ref, pd_ref, *refs)
    half = qq_ref.shape[2]
    rows = st_ref.shape[0]
    pad = jnp.zeros((6, half), F32)
    send_ref[0:128] = o_ref[:, half:]
    send_ref[128:136] = jnp.concatenate([m_ref[:, half:], l_ref[:, half:], pad], axis=0)
    vext = jnp.concatenate([vt_ref[...], jnp.ones((EXT, 128), BF)], axis=0)
    own = dot_t(vext, fk_ref[...])
    send_ref[136 : 136 + rows] = st_ref[...] + jnp.where(c == 0, own, 0.0)
    keep_ref[0:128] = o_ref[:, :half]
    keep_ref[128:136] = jnp.concatenate([m_ref[:, :half], l_ref[:, :half], pad], axis=0)
    keep_ref[136 : 136 + rows] = st_ref[...]


def local_kernel(
    c1, mine_ref, got_ref, q_ref, vt_ref, fq32_ref, fq_ref, fk_ref, num_ref, den_ref,
    y_ref, gq_ref, s_ref, dfk_ref, err_ref,
):
    heads = fq_ref.shape[0] // 128
    rows = 128 + EXT
    v = flip(vt_ref[...]).astype(BF)
    ri = lax.broadcasted_iota(jnp.int32, (128, 128), 0)
    ci = lax.broadcasted_iota(jnp.int32, (128, 128), 1)
    causal = ri <= ci
    hs = range(heads)
    col = [slice(h * 128, (h + 1) * 128) for h in hs]
    state = [mine_ref[136 : 136 + rows, col[h]] + got_ref[136 : 136 + rows, col[h]] for h in hs]
    fq = [fq_ref[col[h]] for h in hs]
    prior = [dot(jnp.concatenate(pieces(state[h], 2), axis=1), jnp.concatenate([fq[h], fq[h]], axis=0)) for h in hs]
    t32 = [state[h][0:128].T for h in hs]
    n32 = [jnp.broadcast_to(state[h][128:129], (128, 128)).T for h in hs]
    total = jnp.zeros((128, 128), F32)
    dnum, dden, dnb = [], [], []
    for h in hs:
        ma, la = mine_ref[128:129, col[h]], mine_ref[129:130, col[h]]
        mb, lb = got_ref[128:129, col[h]], got_ref[129:130, col[h]]
        m = jnp.maximum(ma, mb)
        wa, wb = jnp.exp2((ma - m) * c1), jnp.exp2((mb - m) * c1)
        inv_l = 1.0 / (la * wa + lb * wb)
        teacher = mine_ref[0:128, col[h]] * (wa * inv_l) + got_ref[0:128, col[h]] * (wb * inv_l)
        inv = 1.0 / (den_ref[0:1, col[h]] + prior[h][128:129])
        y = (num_ref[:, col[h]] + prior[h][0:128]) * inv
        y_ref[:, col[h]] = y.T.astype(BF)
        diff = y - teacher
        total = total + diff * diff
        dy = 2.0 * diff
        dnum.append(dy * inv)
        dden.append(-jnp.sum(dy * y, axis=0, keepdims=True) * inv)
        dnb.append(dnum[h].astype(BF))
    dmat = [jnp.where(causal, dot(v, dnb[h]) + dden[h], 0.0).astype(BF) for h in hs]
    for h in hs:
        e = jnp.concatenate(pieces(jnp.broadcast_to(dden[h], (128, 128)), 2), axis=1)
        n = dot_t(jnp.concatenate([fq[h], fq[h]], axis=1), e)
        s_ref[0, col[h]] = dot_t(fq[h], dnb[h]).astype(BF)
        s_ref[1, col[h]], s_ref[2, col[h]] = pieces(n, 2)
    for h in hs:
        dfk_ref[col[h]] = dot_t(fq[h], dmat[h])
    dls = []
    for h in hs:
        t1, t2 = pieces(t32[h], 2)
        d1, d2 = pieces(dnum[h], 2)
        left = jnp.concatenate([fk_ref[col[h]], t1, t1, t2], axis=1)
        right = jnp.concatenate([dmat[h], d1, d2, d1], axis=0)
        dfq = dot(left, right) + n32[h] * dden[h]
        a, b = head_rows(h)
        dls.append((half_grad(fq32_ref[a], dfq[0:64]) - half_grad(fq32_ref[b], dfq[64:128])).astype(BF))
    for h in hs:
        gq_ref[h * 64 : (h + 1) * 64] = dot(dls[h], q_ref[:, col[h]])
    err = jnp.sum(jnp.sum(total, axis=0, keepdims=True), axis=1, keepdims=True)
    err_ref[...] = jnp.broadcast_to(err.reshape(1, 1, 1), err_ref.shape)


def later_kernel(
    cb, nx, idx_ref, s_ref, sp_ref, dfk_ref, pown_ref, k_ref, vt_ref, gq_ref, kz_ref, pz_ref,
    ka_ref, pa_ref, kb_ref, pb_ref, kc_ref, pc_ref, kd_ref, pd_ref, out_ref, g_ref, w_ref, n_ref,
):
    x, z, c = idx_ref[0], idx_ref[1], idx_ref[2]
    heads = dfk_ref.shape[0] // 128
    w_ref[:, 0:128] = s_ref[0]
    w_ref[:, 128:256] = sp_ref[0]
    n_par = sp_ref[1].astype(F32) + sp_ref[2].astype(F32)
    n_ref[...] = (s_ref[1].astype(F32) + s_ref[2].astype(F32)) + n_par
    vt, k = vt_ref[...], k_ref[...]
    dfk = dfk_ref[...] + jnp.where(c == 0, dot(sp_ref[0], vt) + n_par, 0.0)
    parts = []
    for h in range(heads):
        a, b = head_rows(h)
        parts.append(half_grad(pown_ref[a], dfk[a]) - half_grad(pown_ref[b], dfk[b]))
    g_ref[...] = dot(jnp.concatenate(parts, axis=0).astype(BF), k)

    def term(k_ref, p_ref, lead, first, keep=None):
        kc, vc = load_chunk(k_ref, lead, first, cb)
        v2 = jnp.concatenate([vc, vc], axis=0)
        raw = [dot(w_ref[h * 128 : (h + 1) * 128, :], v2) for h in range(heads)]
        out = []
        for h in range(heads):
            bias = n_ref[h * 128 : (h + 1) * 128]
            d = raw[h] + jnp.concatenate([bias] * cb, axis=1)
            a, b = head_rows(h)
            up = jnp.concatenate([p_ref[(*lead, first + i, a)] for i in range(cb)], axis=1)
            down = jnp.concatenate([p_ref[(*lead, first + i, b)] for i in range(cb)], axis=1)
            out.append(half_grad(up, d[0:64]) - half_grad(down, d[64:128]))
        dl = jnp.concatenate(out, axis=0)
        if keep is not None:
            dl = jnp.where(keep(dl.shape), dl, 0.0)
        g_ref[...] += dot(dl.astype(BF), kc)

    def own_slice(i, carry):
        first = i * cb

        def keep(shape):
            return first + lax.broadcasted_iota(jnp.int32, shape, 1) // 128 < z

        term(kz_ref, pz_ref, (), first, keep)
        return carry

    lax.fori_loop(0, (z + cb - 1) // cb, own_slice, 0)

    def earlier(kx_ref, px_ref, valid):
        def step(i, carry):
            term(kx_ref, px_ref, (), i * cb)
            return carry

        lax.fori_loop(0, jnp.where(valid, kx_ref.shape[0] // cb, 0), step, 0)

    earlier(ka_ref, pa_ref, x >= 1)
    earlier(kb_ref, pb_ref, x == nx - 1)
    earlier(kc_ref, pc_ref, x >= 2)
    earlier(kd_ref, pd_ref, x >= 2)
    half = g_ref.shape[0]
    out_ref[0:half] = gq_ref[...].astype(BF)
    out_ref[half : 2 * half] = g_ref[...].astype(BF)


def total_kernel(in_ref, e_ref, out_ref):
    total = jnp.sum(in_ref[...].astype(F32), axis=0)
    pairs = [total[r : r + 2].astype(BF) for r in range(0, total.shape[0], 2)]
    error = jnp.sum(e_ref[:, 0:1, :], axis=0)
    pairs.append(jnp.concatenate(pieces(error, 2), axis=0))
    row = jnp.concatenate(pairs, axis=1)
    out_ref[...] = jnp.broadcast_to(row[None], out_ref.shape)


def last_kernel(count, in_ref, gq_ref, gk_ref, e_ref):
    members, width = in_ref.shape[0], in_ref.shape[2]
    pairs = width // 128 - 1
    half = members // 2
    for i in range(members):
        dst, at = (gq_ref, i) if i < half else (gk_ref, i - half)
        for r in range(pairs):
            row = 2 * (at * pairs + r)
            dst[row : row + 2, :] = in_ref[i, :, r * 128 : (r + 1) * 128].astype(F32)
    error = jnp.sum(in_ref[:, :, pairs * 128 :].astype(F32), axis=0)
    e_ref[...] = jnp.sum(error, axis=0, keepdims=True) / count


def body(queries, keys, values, feat_q, feat_k):
    rows = queries.shape[0]
    heads = feat_q.shape[0]
    hd = keys.shape[1]
    nx, nz = lax.axis_size("x"), lax.axis_size("z")
    nh = lax.axis_size("head")
    nctx = nx * nz * 2
    nhalf = nz // 2
    cb = min(4, nhalf)
    idx = jnp.stack([lax.axis_index("x"), lax.axis_index("z"), lax.axis_index("c")]).astype(jnp.int32)
    c1 = hd**-0.5 * LOG2E
    wide = heads * 128
    srows = 128 + EXT

    def swap(a):
        return lax.ppermute(a, "c", [(0, 1), (1, 0)])

    def move(a, pairs):
        return lax.ppermute(a, "x", pairs)

    wq = jnp.swapaxes(feat_q, 1, 2).reshape(heads * 64, hd)
    wk = jnp.swapaxes(feat_k, 1, 2).reshape(heads * 64, hd)
    qt, kv, vt = call(
        prep_kernel,
        [((hd, wide), BF), ((nz, 2, 128, 128), BF), ((128, 128), BF)],
        tuple(pltpu.with_memory_space_constraint(a, pltpu.HBM) for a in (queries, keys, values)),
        n_hbm=3,
        scratch=[
            pltpu.VMEM((rows, wide), BF),
            pltpu.VMEM((rows, hd), BF),
            pltpu.VMEM((rows, hd), BF),
            pltpu.SemaphoreType.DMA((3,)),
        ],
    )
    kvz = lax.all_to_all(kv, "z", 0, 0, tiled=True)
    ka, kb = move(kvz, [(0, 1), (1, 2), (2, 3)]), move(kvz, [(0, 3), (1, 0)])
    both = lax.all_gather(qt, "c")
    fq32, fq, pown, fk, num, den = call(
        pre_kernel,
        [
            ((wide, 128), F32),
            ((wide, 128), BF),
            ((wide, 128), F32),
            ((wide, 128), BF),
            ((128, wide), F32),
            ((8, wide), F32),
        ],
        (qt, keys, vt, wq, wk),
    )
    carry = [
        ((1, 2 * wide), F32),
        ((1, 2 * wide), F32),
        ((hd, 2 * wide), F32),
        ((srows, wide), F32),
    ]
    m, l, o, st, pz = call(
        functools.partial(own_kernel, c1, cb),
        carry + [((nz, wide, 128), F32)],
        (idx, both, wk, kvz),
        n_smem=1,
    )
    ka, kb, m, fq = lax.optimization_barrier((ka, kb, m, fq))
    kc, kd = move(ka[:nhalf], [(1, 2), (2, 3)]), move(kb[nhalf:], [(3, 2), (0, 3)])
    m, l, o, st, pa, pb = call(
        functools.partial(mid_kernel, c1, cb, nx),
        carry + [((nz, wide, 128), F32)] * 2,
        (idx, both, wk, ka, kb, m, l, o, st),
        n_smem=1,
    )
    mine, send, pc, pd = call(
        functools.partial(end_kernel, c1, cb),
        [((136 + srows, wide), F32)] * 2 + [((nhalf, wide, 128), F32)] * 2,
        (idx, both, wk, kc, kd, m, l, o, st, fk, vt),
        n_smem=1,
        scratch=[pltpu.VMEM(s, d) for s, d in carry],
    )
    got = swap(send)
    student, gq, s, dfk, err = call(
        functools.partial(local_kernel, c1),
        [
            ((rows, wide), BF),
            ((heads * 64, 128), F32),
            ((3, wide, 128), BF),
            ((wide, 128), F32),
            ((nh, 8, 128), F32),
        ],
        (mine, got, queries, vt, fq32, fq, fk, num, den),
    )
    sp = swap(s)
    err = lax.all_to_all(err, "head", 0, 0, tiled=True)
    sp, err = lax.optimization_barrier((sp, err))
    share = 2 * heads * 64 * 128 // nctx
    (out,) = call(
        functools.partial(later_kernel, cb, nx),
        [((2 * heads * 64, 128), BF)],
        (idx, s, sp, dfk, pown, keys, vt, gq, kvz, pz, ka, pa, kb, pb, kc, pc, kd, pd),
        n_smem=1,
        scratch=[
            pltpu.VMEM((heads * 64, 128), F32),
            pltpu.VMEM((wide, 256), BF),
            pltpu.VMEM((wide, 128), F32),
        ],
    )
    arrived = lax.all_to_all(out.reshape(nctx, share // 128, 128), CTX, 0, 0, tiled=True)
    (final,) = call(total_kernel, [((nctx, 2, share // 2 + 128), BF)], (arrived, err))
    final = lax.all_to_all(final, CTX, 0, 0, tiled=True)
    gq, gk, error = call(
        functools.partial(last_kernel, float(nctx * nh * rows * wide)),
        [((heads * 64, 128), F32)] * 2 + [((1, 128), F32)],
        (final,),
    )
    gq, gk = (jnp.swapaxes(g.reshape(heads, 64, 128), 1, 2) for g in (gq, gk))
    return student, gq, gk, error[0, 0]


def solution(mesh):
    nctx = mesh.shape["ctx"]
    split = Mesh(
        mesh.devices.reshape(4, nctx // 8, 2, mesh.shape["head"]), ("x", "z", "c", "head")
    )
    in_specs = (
        P(CTX, "head"),
        P(CTX, "head"),
        P(CTX, "head"),
        P("head", None, None),
        P("head", None, None),
    )
    out_specs = (P(CTX, "head"), P("head", None, None), P("head", None, None), P())
    return jax.shard_map(body, mesh=split, in_specs=in_specs, out_specs=out_specs, check_vma=False)
```
